32 devices in a mesh: dp: 16 (over z, y, x), mp: 2 (over core).
Axes of the slice: x: 2, y: 2, z: 4, core: 2. Of those that a mesh axis runs over, the one named last changes fastest.
Arguments:
- layer_in: bfloat16 [16384, 768], P('dp'), may hold values from -6 to 6
- memory: bfloat16 [32, 512, 768], P('dp'), may hold values from -6 to 6
- grad_out: bfloat16 [16384, 768], P('dp'), may hold values from -6 to 6
- seq_len: int32 [32], P('dp'), may hold values from 129 to 512, as said below
- rel_bucket: int32 [512, 512], replicated, may hold values from 0 to 31
- self_gain: float32 [768], replicated, may hold values from 0.5 to 1.5
- cross_gain: float32 [768], replicated, may hold values from 0.5 to 1.5
- ffn_gain: float32 [768], replicated, may hold values from 0.5 to 1.5
- rel_table: float32 [32, 12], P(None, 'mp'), may hold values from -4 to 4
- self_q: bfloat16 [768, 768], P(None, 'mp'), may hold values from -0.0546875 to 0.0546875
- self_kv: bfloat16 [768, 2, 768], P(None, None, 'mp'), may hold values from -0.21875 to 0.21875
- self_o: bfloat16 [768, 768], P('mp'), may hold values from -0.875 to 0.875
- cross_q: bfloat16 [768, 768], P(None, 'mp'), may hold values from -0.0546875 to 0.0546875
- cross_kv: bfloat16 [768, 2, 768], P(None, None, 'mp'), may hold values from -0.21875 to 0.21875
- cross_o: bfloat16 [768, 768], P('mp'), may hold values from -0.875 to 0.875
- ffn_in: bfloat16 [768, 2, 2048], P(None, None, 'mp'), may hold values from -0.21875 to 0.21875
- ffn_out: bfloat16 [2048, 768], P('mp'), may hold values from -0.125 to 0.125
Outputs:
- mixed: bfloat16 [16384, 768], P('dp', 'mp')
- grad_layer_in: float32 [16384, 768], P('dp')
- grad_memory: float32 [32, 512, 768], P('dp', None, 'mp')
- grad_self_gain: float32 [768], P('dp')
- grad_cross_gain: float32 [768], P('dp')
- grad_ffn_gain: float32 [768], P('dp')
- grad_rel_table: float32 [32, 12], P(None, 'mp')
- grad_self_q: float32 [768, 768], P('dp', 'mp')
- grad_self_kv: float32 [768, 2, 768], P('dp', None, 'mp')
- grad_self_o: float32 [768, 768], P('mp', 'dp')
- grad_cross_q: float32 [768, 768], P('dp', 'mp')
- grad_cross_kv: float32 [768, 2, 768], P('dp', None, 'mp')
- grad_cross_o: float32 [768, 768], P('mp', 'dp')
- grad_ffn_in: float32 [768, 2, 2048], P('dp', None, 'mp')
- grad_ffn_out: float32 [2048, 768], P('mp', 'dp')
The draws below stay inside these ranges and needn't reach their ends.
Inputs may be any that keep to these rules, and one draw needn't show every extreme that they name: Slots of a sequence at or past its seq_len are padding that no query attends to; sequence 0 has 512 targets.
All inputs are finite; a program needn't handle non-finite values.
Results may differ from the reference program's by a relative error of at most 0.022.
The reference program's roundings to bfloat16 on the way count: a program that leaves them out, or rounds other values in their place, can miss the bound.
Values sent between devices are 32-bit elements; how exact they have to be, the bound alone decides.
No kernel may reach another device: no remote copies, remote signals or barrier semaphores. Data moves between devices by JAX's collectives and lax.ppermute only.
A program may use at most 192 MiB of HBM per device.

```python
import jax
import jax.numpy as jnp
from jax import lax

D = 768
H = 12
DH = 64
FF = 2048
NB = 32
L = 512
ENC = 512
HD = 768
SEQUENCES = 32
TOKENS = 16384


def draw_seq_len(key, part):
    first, second, third = jax.random.split(key, 3)
    longer = jax.random.randint(first, (SEQUENCES,), 0, 2)
    short_len = jax.random.randint(second, (SEQUENCES,), L // 4 + 1, L // 2 + 1)
    long_len = jax.random.randint(third, (SEQUENCES,), L // 2 + 1, L + 1)
    lengths = jnp.where(longer == 1, long_len, short_len)
    return lengths.at[0].set(L).astype(jnp.int32)


def plant(array, own_key, low, high):
    place = [jax.random.randint(jax.random.fold_in(own_key, axis), (), 0, length) for axis, length in enumerate(array.shape)]
    widest = array.shape.index(max(array.shape))
    next_to = place[:widest] + [(place[widest] + 1) % array.shape[widest]] + place[widest + 1:]
    return array.at[tuple(place)].set(low).at[tuple(next_to)].set(high)


def levels(key, shape, pieces, least, high):
    def one(position, parts):
        heights = jax.random.uniform(jax.random.fold_in(jax.random.fold_in(key, 6), position), (parts,), jnp.float32, least / len(pieces), high / len(pieces))
        return jnp.repeat(jnp.exp(heights), shape[position] // parts).reshape((-1,) + (1,) * (len(shape) - position - 1))

    level = one(*pieces[0])
    for cut in pieces[1:]:
        level = level * one(*cut)
    return level


def scatter_about(rng, extent, deviation, bound, shards=(), kind=jnp.bfloat16):
    values = deviation * jax.random.normal(rng, extent, jnp.float32)
    if shards:
        values = values * levels(rng, extent, shards, -0.22, 0.18)
    return jnp.clip(values, -bound, bound).astype(kind)


def setup_inputs(seed: int = 0) -> dict:
    seeds = jax.random.split(jax.random.key(seed), 18)
    layer_in = scatter_about(seeds[0], (TOKENS, D), 1.0, 6.0, ((0, 16),))
    memory = scatter_about(seeds[1], (SEQUENCES, ENC, D), 1.0, 6.0, ((0, 16),))
    grad_out = scatter_about(seeds[2], (TOKENS, D), 1.0, 6.0, ((0, 16),))
    seq_len = draw_seq_len(jax.random.fold_in(seeds[17], 71), 0)
    rel_bucket = plant(jax.random.randint(seeds[4], (L, L), 0, NB), jax.random.fold_in(seeds[4], 1), 0, NB - 1).astype(jnp.int32)
    self_gain = jnp.clip(1.0 + 0.1 * jax.random.normal(seeds[5], (D,), jnp.float32), 0.5, 1.5)
    cross_gain = jnp.clip(1.0 + 0.1 * jax.random.normal(seeds[6], (D,), jnp.float32), 0.5, 1.5)
    ffn_gain = jnp.clip(1.0 + 0.1 * jax.random.normal(seeds[7], (D,), jnp.float32), 0.5, 1.5)
    rel_table = scatter_about(seeds[8], (NB, H), 1.0, 4.0, ((1, 2),), jnp.float32)
    self_q = scatter_about(seeds[9], (D, HD), (16 * D) ** -0.5, 0.0546875, ((1, 2),))
    self_kv = scatter_about(seeds[10], (D, 2, HD), D ** -0.5, 0.21875, ((2, 2),))
    self_o = scatter_about(seeds[11], (HD, D), (HD // 16) ** -0.5, 0.875, ((0, 2),))
    cross_q = scatter_about(seeds[12], (D, HD), (16 * D) ** -0.5, 0.0546875, ((1, 2),))
    cross_kv = scatter_about(seeds[13], (D, 2, HD), D ** -0.5, 0.21875, ((2, 2),))
    cross_o = scatter_about(seeds[14], (HD, D), (HD // 16) ** -0.5, 0.875, ((0, 2),))
    ffn_in = scatter_about(seeds[15], (D, 2, FF), D ** -0.5, 0.21875, ((2, 2),))
    ffn_out = scatter_about(seeds[16], (FF, D), FF ** -0.5, 0.125, ((0, 2),))
    return dict(layer_in=layer_in, memory=memory, grad_out=grad_out, seq_len=seq_len, rel_bucket=rel_bucket, self_gain=self_gain, cross_gain=cross_gain, ffn_gain=ffn_gain, rel_table=rel_table, self_q=self_q, self_kv=self_kv, self_o=self_o, cross_q=cross_q, cross_kv=cross_kv, cross_o=cross_o, ffn_in=ffn_in, ffn_out=ffn_out)


EPS = 1e-06
NEGATIVE = -1e+30
HIGHEST = lax.Precision.HIGHEST

@jax.custom_vjp
def low(v):
    return lax.optimization_barrier(v.astype(jnp.bfloat16)).astype(jnp.float32)

@jax.custom_vjp
def low_back(v):
    return v

def low_keep(v):
    return (low(v), None)

def low_pass(kept, grad):
    return (grad,)

def back_keep(v):
    return (v, None)

def back_low(kept, grad):
    return (low(grad),)
low.defvjp(low_keep, low_pass)
low_back.defvjp(back_keep, back_low)

def rounded(v):
    return low_back(low(v))

def rms(values, gain):
    return values * lax.rsqrt(lax.optimization_barrier(jnp.mean(values * values, axis=-1, keepdims=True)) + EPS) * gain

def mix(form, first, second):
    return jnp.einsum(form, first, second, precision=HIGHEST)

def attention(query, keys, values, bias, valid):
    raw = mix('qhd,khd->hqk', query, keys)
    if bias is not None:
        raw = raw + bias
    raw = low_back(raw)
    if valid is not None:
        raw = jnp.where(valid, raw, NEGATIVE)
    probs = low(jax.nn.softmax(raw, axis=-1))
    return mix('hqk,khd->qhd', probs, values)

def reference(layer_in, memory, grad_out, seq_len, rel_bucket, self_gain, cross_gain, ffn_gain, rel_table, self_q, self_kv, self_o, cross_q, cross_kv, cross_o, ffn_in, ffn_out):
    positions = jnp.arange(L, dtype=jnp.int32)
    causal = positions[None, :] <= positions[:, None]

    def forward(inputs, encoded, gain_one, gain_two, gain_three, table, wq1, wkv1, wo1, wq2, wkv2, wo2, w_in, w_out):
        normed1 = low(rms(inputs, gain_one))
        query1 = rounded(mix('td,dh->th', normed1, wq1)).reshape(SEQUENCES, L, H, DH)
        pair1 = rounded(mix('td,dch->tch', normed1, wkv1))
        keys1 = pair1[:, 0].reshape(SEQUENCES, L, H, DH)
        values1 = pair1[:, 1].reshape(SEQUENCES, L, H, DH)
        bias = jnp.transpose(table[rel_bucket], (2, 0, 1))

        def self_one(item):
            query, keys, values, count = item
            valid = causal & (positions[None, :] < count)
            return attention(query, keys, values, bias, valid[None])
        context1 = lax.map(jax.checkpoint(self_one), (query1, keys1, values1, seq_len))
        context1 = rounded(context1.reshape(TOKENS, HD))
        hidden1 = inputs + low_back(mix('th,hd->td', context1, wo1))
        normed2 = low(rms(hidden1, gain_two))
        query2 = rounded(mix('td,dh->th', normed2, wq2)).reshape(SEQUENCES, L, H, DH)
        pair2 = rounded(mix('sed,dch->sech', encoded, wkv2))
        keys2 = pair2[:, :, 0].reshape(SEQUENCES, ENC, H, DH)
        values2 = pair2[:, :, 1].reshape(SEQUENCES, ENC, H, DH)

        def cross_one(item):
            query, keys, values = item
            return attention(query, keys, values, None, None)
        context2 = lax.map(jax.checkpoint(cross_one), (query2, keys2, values2))
        context2 = rounded(context2.reshape(TOKENS, HD))
        hidden2 = hidden1 + low_back(mix('th,hd->td', context2, wo2))
        normed3 = low(rms(hidden2, gain_three))
        gate_up = low_back(mix('td,dcf->tcf', normed3, w_in))
        inner = low(jax.nn.gelu(gate_up[:, 0], approximate=True) * gate_up[:, 1])
        return hidden2 + low_back(mix('tf,fd->td', inner, w_out))
    primals = (layer_in.astype(jnp.float32), memory.astype(jnp.float32), self_gain, cross_gain, ffn_gain, rel_table, self_q.astype(jnp.float32), self_kv.astype(jnp.float32), self_o.astype(jnp.float32), cross_q.astype(jnp.float32), cross_kv.astype(jnp.float32), cross_o.astype(jnp.float32), ffn_in.astype(jnp.float32), ffn_out.astype(jnp.float32))
    result, pull = jax.vjp(forward, *primals)
    grads = pull(grad_out.astype(jnp.float32))
    return (result.astype(jnp.bfloat16), grads[0], grads[1], grads[2], grads[3], grads[4], grads[5], grads[6], grads[7], grads[8], grads[9], grads[10], grads[11], grads[12], grads[13])
```

```python
import functools

import jax
import jax.numpy as jnp
from jax import lax
from jax.experimental import pallas as pl
from jax.experimental.pallas import tpu as pltpu
from jax.sharding import PartitionSpec as P

EPS = 1e-06
NEGATIVE = -1e30
F32 = jnp.float32
BF16 = jnp.bfloat16
LANES = 128
QB = 128


def nn(left, right):
    return lax.dot_general(left, right, (((1,), (0,)), ((), ())), preferred_element_type=F32)


def nt(left, right):
    return lax.dot_general(left, right, (((1,), (1,)), ((), ())), preferred_element_type=F32)


def norm(values, gain):
    inverse = lax.rsqrt(jnp.mean(values * values, axis=-1, keepdims=True) + EPS)
    scaled = values * inverse
    return scaled * gain, scaled, inverse


def norm_back(grad, values, gain):
    inverse = lax.rsqrt(jnp.mean(values * values, axis=-1, keepdims=True) + EPS)
    scaled = values * inverse
    grad_scaled = grad * gain
    inner = jnp.mean(grad_scaled * scaled, axis=-1, keepdims=True)
    gain_grad = jnp.sum(grad * scaled, axis=0, keepdims=True)
    return inverse * (grad_scaled - scaled * inner), gain_grad


def own_half(value, side):
    lane = lax.broadcasted_iota(jnp.int32, value.shape, 1)
    keep = lane < LANES // 2 if side == 0 else lane >= LANES // 2
    return jnp.where(keep, value, jnp.zeros_like(value))


def join_halves(first, second):
    lane = lax.broadcasted_iota(jnp.int32, first.shape, 1)
    return jnp.where(lane < LANES // 2, first, second)


def bias_of(table_ref, bucket_ref, head, start, rows, keys):
    row = jnp.broadcast_to(table_ref[pl.ds(head, 1), :], (rows, LANES))
    parts = []
    for first in range(0, keys, LANES):
        index = bucket_ref[start : start + rows, first : first + LANES]
        parts.append(jnp.take_along_axis(row, index, axis=1, mode="promise_in_bounds"))
    return jnp.concatenate(parts, axis=1) if len(parts) > 1 else parts[0]


def masked(raw, start, count):
    rows, keys = raw.shape
    place = lax.broadcasted_iota(jnp.int32, (rows, 1), 0) + (start + 1)
    limit = jnp.minimum(place, count)
    column = lax.broadcasted_iota(jnp.int32, raw.shape, 1)
    return jnp.where(column < limit, raw, NEGATIVE)


def attend(q_ref, k_ref, v_ref, c_ref, lse_ref, length, keys_all, score):
    pairs = q_ref.shape[1] // LANES
    lane = lax.broadcasted_iota(jnp.int32, (QB, LANES), 1)

    def one_pair(pair, carry):
        columns = pl.ds(pl.multiple_of(pair * LANES, LANES), LANES)
        for start in range(0, length, QB):
            keys = keys_all(start)
            query = q_ref[start : start + QB, columns]
            key = k_ref[0:keys, columns]
            value = v_ref[0:keys, columns]
            found = []
            kept = lse_ref[start : start + QB, :]
            for side in range(2):
                head = pair * 2 + side
                raw = score(nt(own_half(query, side), key), head, start)
                top = jnp.max(raw, axis=1, keepdims=True)
                weight = jnp.exp(raw - top)
                total = jnp.sum(weight, axis=1, keepdims=True)
                probs = (weight * (1.0 / total)).astype(BF16)
                found.append(nn(probs, value))
                kept = jnp.where(lane == head, top + jnp.log(total), kept)
            lse_ref[start : start + QB, :] = kept
            c_ref[start : start + QB, columns] = join_halves(*found).astype(BF16)
        return carry

    lse_ref[...] = jnp.zeros_like(lse_ref)
    lax.fori_loop(0, pairs, one_pair, 0)


def attend_back(q_ref, k_ref, v_ref, dc_ref, lse_ref, d_ref, qt, dct, dkt, dvt, ds_ref, length, keys_all, score):
    width = q_ref.shape[1]
    pairs = width // LANES
    lane = lax.broadcasted_iota(jnp.int32, (QB, LANES), 1)
    qt[...] = q_ref[...].T
    dct[...] = dc_ref[...].T
    half = LANES // 2

    def one_pair(pair, carry):
        columns = pl.ds(pl.multiple_of(pair * LANES, LANES), LANES)
        for start in range(0, length, QB):
            rows = slice(start, start + QB)
            keys = keys_all(start)
            query = q_ref[rows, columns]
            grad = dc_ref[rows, columns]
            key = k_ref[0:keys, columns]
            value = v_ref[0:keys, columns]
            lse_all = lse_ref[rows, :]
            found = []
            for side in range(2):
                head = pair * 2 + side
                lse = jnp.sum(jnp.where(lane == head, lse_all, 0.0), axis=1, keepdims=True)
                raw = score(nt(own_half(query, side), key), head, start)
                probs = jnp.exp(raw - lse)
                grad_probs = nt(own_half(grad, side), value)
                inner = jnp.sum(probs * grad_probs, axis=1, keepdims=True)
                low = probs.astype(BF16)
                grad_raw = (probs * (grad_probs - inner)).astype(BF16)
                if ds_ref is not None:
                    ds_ref[pl.ds(head, 1), rows, 0:keys] = grad_raw[None]
                found.append(nn(grad_raw, key))
                place = pl.ds(pl.multiple_of(pair * LANES + side * half, half), half)
                add_k = nn(qt[place, rows], grad_raw)
                add_v = nn(dct[place, rows], low)
                if start == 0:
                    dkt[place, 0:keys] = add_k
                    dvt[place, 0:keys] = add_v
                else:
                    before = keys_all(start - QB)
                    dkt[place, 0:before] += add_k[:, 0:before]
                    dvt[place, 0:before] += add_v[:, 0:before]
                    if before < keys:
                        dkt[place, before:keys] = add_k[:, before:keys]
                        dvt[place, before:keys] = add_v[:, before:keys]
            d_ref[rows, columns] = join_halves(*found).astype(BF16)
        return carry

    lax.fori_loop(0, pairs, one_pair, 0)
    d_ref[:, width : 2 * width] = dkt[...].astype(BF16).T
    d_ref[:, 2 * width : 3 * width] = dvt[...].astype(BF16).T


def causal_keys(start):
    return start + QB


def self_forward(len_ref, x_ref, gain_ref, wq_ref, wkv_ref, wo_ref, table_ref, bucket_ref,
                 part_ref, n_ref, qkv_ref, c_ref, lse_ref, *, seq, width):
    length = x_ref.shape[0]
    normed, _, _ = norm(x_ref[...].astype(F32), gain_ref[...])
    n_ref[...] = normed.astype(BF16)
    qkv_ref[:, 0:width] = nn(n_ref[...], wq_ref[...]).astype(BF16)
    qkv_ref[:, width:] = nn(n_ref[...], wkv_ref[...]).astype(BF16)
    count = len_ref[seq]

    def score(raw, head, start):
        biased = raw + bias_of(table_ref, bucket_ref, head, start, *raw.shape)
        return masked(biased, start, count)

    attend(qkv_ref.at[:, 0:width], qkv_ref.at[:, width : 2 * width], qkv_ref.at[:, 2 * width : 3 * width],
           c_ref, lse_ref, length, causal_keys, score)
    part_ref[...] = nn(c_ref[...], wo_ref[...])


def project(x_ref, w_ref, out_ref):
    out_ref[...] = nn(x_ref[...], w_ref[...]).astype(out_ref.dtype)


def cross_forward(x_ref, mine_ref, theirs_ref, gain_ref, wq_ref, wo_ref, kv_ref,
                  part_ref, h_ref, n_ref, q_ref, c_ref, lse_ref, *, width):
    hidden = x_ref[...].astype(F32) + (mine_ref[...] + theirs_ref[...])
    h_ref[...] = hidden
    normed, _, _ = norm(hidden, gain_ref[...])
    n_ref[...] = normed.astype(BF16)
    q_ref[...] = nn(n_ref[...], wq_ref[...]).astype(BF16)
    keys = kv_ref.shape[0]
    attend(q_ref, kv_ref.at[:, 0:width], kv_ref.at[:, width : 2 * width], c_ref, lse_ref,
           x_ref.shape[0], lambda start: keys, lambda raw, head, start: raw)
    part_ref[...] = nn(c_ref[...], wo_ref[...])


GELU_C = 0.7978845608028654
GELU_A = 0.044715


def ffn_both(side_ref, h_ref, mine_ref, theirs_ref, gain_ref, dy_ref, win_ref, wout_ref,
             mixed_ref, other_ref, h2_ref, n_ref, inner_ref, dgu_ref, dn_ref, scratch):
    hidden = h_ref[...] + (mine_ref[...] + theirs_ref[...])
    h2_ref[...] = hidden
    normed, _, _ = norm(hidden, gain_ref[...])
    n_ref[...] = normed.astype(BF16)
    units = wout_ref.shape[0]
    step = 256

    def one(chunk, carry):
        first = pl.multiple_of(chunk * step, step)
        here = pl.ds(first, step)
        there = pl.ds(pl.multiple_of(units + chunk * step, step), step)
        gate = nn(n_ref[...], win_ref[:, here])
        upward = nn(n_ref[...], win_ref[:, there])
        grad = nt(dy_ref[...], wout_ref[here, :])
        squared = gate * gate
        bent = jnp.tanh(gate * (GELU_C + (GELU_C * GELU_A) * squared))
        half = 0.5 + 0.5 * bent
        soft = gate * half
        slope = half + (0.5 * gate) * (1.0 - bent * bent) * (GELU_C + (3 * GELU_C * GELU_A) * squared)
        inner_ref[:, here] = (soft * upward).astype(BF16)
        dgu_ref[:, here] = (grad * upward * slope).astype(BF16)
        dgu_ref[:, there] = (grad * soft).astype(BF16)
        return carry

    lax.fori_loop(0, units // step, one, 0)
    dn_ref[...] = nt(dgu_ref[...], win_ref[...])
    share = nn(inner_ref[...], wout_ref[...])
    scratch[...] = share
    half = mixed_ref.shape[1]
    me = side_ref[0]
    mine = pl.ds(pl.multiple_of(me * half, LANES), half)
    other = pl.ds(pl.multiple_of((1 - me) * half, LANES), half)
    mixed_ref[...] = h2_ref[:, mine] + scratch[:, mine]
    other_ref[...] = scratch[:, other]


def cross_backward(side_ref, dy_ref, mine_ref, theirs_ref, h_ref, gain_ref, q_ref, kv_ref, lse_ref,
                   wq_ref, wkv_ref, wo_ref,
                   dn_ref, dh_ref, da_ref, d_ref, gm_ref, go_ref, gain_out_ref,
                   dc, qt, dct, dkt, dvt, scratch, *, width):
    back, gain_grad = norm_back(mine_ref[...] + theirs_ref[...], h_ref[...], gain_ref[...])
    gain_out_ref[...] = gain_grad
    grad = dy_ref[...].astype(F32) + back
    dh_ref[...] = grad
    da_ref[...] = grad.astype(BF16)
    dc[...] = nt(da_ref[...], wo_ref[...]).astype(BF16)
    keys = kv_ref.shape[0]
    attend_back(q_ref, kv_ref.at[:, 0:width], kv_ref.at[:, width : 2 * width], dc, lse_ref, d_ref,
                qt, dct, dkt, dvt, None, dy_ref.shape[0], lambda start: keys, lambda raw, head, start: raw)
    dn_ref[...] = nt(d_ref[:, 0:width], wq_ref[...])
    scratch[...] = nt(d_ref[:, width : 3 * width], wkv_ref[...])
    half = gm_ref.shape[1]
    me = side_ref[0]
    gm_ref[...] = scratch[:, pl.ds(pl.multiple_of(me * half, LANES), half)]
    go_ref[...] = scratch[:, pl.ds(pl.multiple_of((1 - me) * half, LANES), half)]


def self_backward(len_ref, before_ref, mine_ref, theirs_ref, h_ref, gain_ref, qkv_ref, lse_ref,
                  wq_ref, wkv_ref, wo_ref, table_ref, bucket_ref,
                  dn_ref, dh_ref, da_ref, d_ref, ds_ref, gain_out_ref,
                  dc, qt, dct, dkt, dvt, *, seq, width):
    back, gain_grad = norm_back(mine_ref[...] + theirs_ref[...], h_ref[...], gain_ref[...])
    gain_out_ref[...] = gain_grad
    grad = before_ref[...] + back
    dh_ref[...] = grad
    da_ref[...] = grad.astype(BF16)
    dc[...] = nt(da_ref[...], wo_ref[...]).astype(BF16)
    count = len_ref[seq]

    def score(raw, head, start):
        biased = raw + bias_of(table_ref, bucket_ref, head, start, *raw.shape)
        return masked(biased, start, count)

    attend_back(qkv_ref.at[:, 0:width], qkv_ref.at[:, width : 2 * width], qkv_ref.at[:, 2 * width : 3 * width],
                dc, lse_ref, d_ref, qt, dct, dkt, dvt, ds_ref, h_ref.shape[0], causal_keys, score)
    dn_ref[...] = nt(d_ref[:, 0:width], wq_ref[...]) + nt(d_ref[:, width : 3 * width], wkv_ref[...])


def input_backward(before_ref, mine_ref, theirs_ref, x_ref, gain_ref, out_ref, gain_out_ref):
    back, gain_grad = norm_back(mine_ref[...] + theirs_ref[...], x_ref[...].astype(F32), gain_ref[...])
    gain_out_ref[...] = gain_grad
    out_ref[...] = before_ref[...] + back


def table_backward(bucket_ref, first_ref, second_ref, out_ref, total, *, buckets):
    heads, length, _ = first_ref.shape
    group = 8

    def one(block, carry):
        start = pl.multiple_of(block * group, group)
        rows = pl.ds(start, group)
        code = bucket_ref[rows, :]
        spread = lax.broadcasted_iota(jnp.int32, (buckets, length), 0)
        column = lax.broadcasted_iota(jnp.int32, (1, length), 1)
        pieces = []
        for i in range(group):
            seen = jnp.where(column <= start + i, code[i : i + 1, :], -1)
            pieces.append((spread == seen).astype(F32))
        chosen = jnp.concatenate(pieces, axis=0).astype(BF16)
        for ref in (first_ref, second_ref):
            values = ref[:, rows, :].astype(F32)
            values = jnp.where(column[None] <= start + group - 1, values, 0.0)
            values = values.reshape(heads * group, length).astype(BF16)
            total[...] += nt(values, chosen)
        return carry

    total[...] = jnp.zeros_like(total)
    lax.fori_loop(0, length // group, one, 0)
    row = lax.broadcasted_iota(jnp.int32, total.shape, 0)
    column = lax.broadcasted_iota(jnp.int32, total.shape, 1)
    out_ref[...] = jnp.where(lax.rem(row, group) == column // buckets, total[...], 0.0)


def weight_grad(index_ref, l0_ref, l1_ref, r0_ref, r1_ref, *rest, stride, blocks):
    outs, (turned, scratch) = rest[:-2], rest[-2:]
    length = l0_ref.shape[0]

    @pl.when(pl.program_id(0) == 0)
    def _():
        turned[:, 0:length] = l0_ref[...].T
        turned[:, length : 2 * length] = l1_ref[...].T

    value = nn(turned[:, 0:length], r0_ref[...]) + nn(turned[:, length : 2 * length], r1_ref[...])
    if stride is None:
        outs[0][...] = value
        return
    scratch[...] = value
    keep_ref, send_ref = outs
    block = scratch.shape[0] // blocks
    bit = lax.rem(index_ref[0] // stride, 2)
    for place in range(blocks // 2):
        low, high = place % stride, place // stride
        base = high * 2 * stride + low
        mine = pl.multiple_of((base + bit * stride) * block, 8)
        other = pl.multiple_of((base + (1 - bit) * stride) * block, 8)
        keep_ref[place] = scratch[pl.ds(mine, block), :]
        send_ref[place] = scratch[pl.ds(other, block), :]


def call(body, name, outs, args, scratch=(), smem=0, flops=0, spent=0):
    def spec(value):
        shape = value.shape
        return pl.BlockSpec(shape, lambda i: (0,) * len(shape), pipeline_mode=pl.Buffered(1))

    in_specs, arrays = [], []
    for place, value in enumerate(args):
        if place < smem:
            in_specs.append(pl.BlockSpec(memory_space=pltpu.SMEM))
            arrays.append(value)
        elif isinstance(value, tuple):
            array, size, block = value
            shape = (size,) + array.shape[1:]
            rest = (0,) * (array.ndim - 1)
            in_specs.append(
                pl.BlockSpec(
                    shape,
                    lambda i, block=block, rest=rest: (block,) + rest,
                    pipeline_mode=pl.Buffered(1),
                )
            )
            arrays.append(array)
        else:
            in_specs.append(spec(value))
            arrays.append(value)
    moved = sum(o.size * o.dtype.itemsize for o in outs) + sum(a.size * a.dtype.itemsize for a in arrays)
    return pl.pallas_call(
        body,
        name=name,
        grid=(1,),
        out_shape=outs,
        in_specs=in_specs,
        out_specs=[spec(o) for o in outs],
        scratch_shapes=list(scratch),
        compiler_params=pltpu.CompilerParams(vmem_limit_bytes=48 * 2**20),
        cost_estimate=pl.CostEstimate(flops=flops, bytes_accessed=moved, transcendentals=spent),
    )(*arrays)


def shape(dims, dtype):
    return jax.ShapeDtypeStruct(dims, dtype)


def swap(value):
    size = lax.axis_size("mp")
    return lax.ppermute(value, "mp", [(i, size - 1 - i) for i in range(size)])


def dp_sum(value):
    count = lax.axis_size("dp")
    bit = 1
    while bit < count:
        value = value + lax.ppermute(value, "dp", [(i, i ^ bit) for i in range(count)])
        bit *= 2
    return value


def weight_part(index, lefts, rights, order, name):
    count = lax.axis_size("dp")
    length, model = lefts[0].shape
    columns = rights[0].shape[1]
    block = model // count
    direct = block % 8 == 0 and count > 1
    step = 384 if columns % 384 == 0 else 512
    if direct:
        outs = [shape((count // 2, block, columns), F32)] * 2
        out_specs = [pl.BlockSpec((count // 2, block, step), lambda j: (0, 0, j))] * 2
    else:
        outs = [shape((model, columns), F32)]
        out_specs = [pl.BlockSpec((model, step), lambda j: (0, j))]
    whole = lambda j: (0, 0)
    found = pl.pallas_call(
        functools.partial(weight_grad, stride=order[0] if direct else None, blocks=count),
        name=name,
        grid=(columns // step,),
        out_shape=outs,
        in_specs=[pl.BlockSpec(memory_space=pltpu.SMEM)]
        + [pl.BlockSpec((length, model), whole)] * 2
        + [pl.BlockSpec((length, step), lambda j: (0, j))] * 2,
        out_specs=out_specs,
        scratch_shapes=[pltpu.VMEM((model, 2 * length), BF16), pltpu.VMEM((model, step), F32)],
        compiler_params=pltpu.CompilerParams(vmem_limit_bytes=48 * 2**20),
        cost_estimate=pl.CostEstimate(
            flops=4 * length * model * columns,
            bytes_accessed=4 * model * columns + 4 * length * (model + columns),
            transcendentals=0,
        ),
    )(index, *lefts, *rights)
    if not direct:
        return lax.psum_scatter(found[0], "dp", scatter_dimension=0, tiled=True)
    keep, send = found
    left = [bit for bit in sorted(order) if bit != order[0]]
    arrived = lax.ppermute(send, "dp", [(i, i ^ order[0]) for i in range(count)])
    total = keep + arrived
    for stride in order[1:]:
        low = 2 ** left.index(stride)
        left.remove(stride)
        bit = lax.rem(index[0] // stride, 2)
        split = total.reshape(-1, 2, low, block, columns)
        mine = lax.dynamic_index_in_dim(split, bit, 1, keepdims=False)
        other = lax.dynamic_index_in_dim(split, 1 - bit, 1, keepdims=False)
        arrived = lax.ppermute(other, "dp", [(i, i ^ stride) for i in range(count)])
        total = mine + arrived
    return total.reshape(block, columns)


def orders(count):
    bits = []
    bit = 1
    while bit < count:
        bits.append(bit)
        bit *= 2
    if len(bits) != 4:
        return bits, bits, bits
    return [1, 2, 4, 8], [2, 1, 4, 8], [4, 8, 1, 2]


def on_device(
    layer_in,
    memory,
    grad_out,
    seq_len,
    rel_bucket,
    self_gain,
    cross_gain,
    ffn_gain,
    rel_table,
    self_q,
    self_kv,
    self_o,
    cross_q,
    cross_kv,
    cross_o,
    ffn_in,
    ffn_out,
):
    buckets, heads = rel_table.shape
    width = self_q.shape[1]
    length = rel_bucket.shape[0]
    encoded = memory.shape[1]
    model = layer_in.shape[1]
    units = ffn_out.shape[0]
    seqs = seq_len.shape[0]
    half = model // lax.axis_size("mp")
    count = lax.axis_size("dp")
    side = lax.axis_index("mp").astype(jnp.int32).reshape(1)
    index = lax.axis_index("dp").astype(jnp.int32).reshape(1)
    table = jnp.zeros((8, LANES), F32).at[:heads, :buckets].set(rel_table.T)
    kv1 = self_kv.reshape(model, 2 * width)
    kv2 = cross_kv.reshape(model, 2 * width)
    w_in = ffn_in.reshape(model, 2 * units)
    gains = [g.reshape(1, model) for g in (self_gain, cross_gain, ffn_gain)]
    encoder = memory.reshape(seqs * encoded, model)
    first_order, second_order, third_order = orders(count)
    across = range(seqs)
    rows = lambda array, s: (array, length, s)
    scores = 4 * length * length * LANES * heads

    stage1 = []
    for s in across:
        stage1.append(call(
            functools.partial(self_forward, seq=s, width=width), "self_forward",
            [shape((length, model), F32), shape((length, model), BF16), shape((length, 3 * width), BF16),
             shape((length, width), BF16), shape((length, LANES), F32)],
            [seq_len, rows(layer_in, s), gains[0], self_q, kv1, self_o, table, rel_bucket],
            smem=1, flops=8 * length * model * width + scores, spent=length * length * heads,
        ))
    swapped1 = [swap(found[0]) for found in stage1]
    encoded_kv = [
        call(project, "encoder_kv", [shape((encoded, 2 * width), BF16)], [(encoder, encoded, s), kv2],
             flops=4 * encoded * model * width)[0]
        for s in across
    ]
    stage2 = []
    for s in across:
        stage2.append(call(
            functools.partial(cross_forward, width=width), "cross_forward",
            [shape((length, model), F32), shape((length, model), F32), shape((length, model), BF16),
             shape((length, width), BF16), shape((length, width), BF16), shape((length, LANES), F32)],
            [rows(layer_in, s), stage1[s][0], swapped1[s], gains[1], cross_q, cross_o, encoded_kv[s]],
            flops=4 * length * model * width + scores, spent=length * length * heads,
        ))
    swapped2 = [swap(found[0]) for found in stage2]
    stage3 = []
    for s in across:
        stage3.append(call(
            ffn_both, "ffn_both",
            [shape((length, half), F32), shape((length, half), F32), shape((length, model), F32),
             shape((length, model), BF16), shape((length, units), BF16), shape((length, 2 * units), BF16),
             shape((length, model), F32)],
            [side, stage2[s][1], stage2[s][0], swapped2[s], gains[2], rows(grad_out, s), w_in, ffn_out],
            scratch=[pltpu.VMEM((length, model), F32)],
            smem=1, flops=12 * length * model * units, spent=length * units,
        ))
    swapped3 = [swap(found[6]) for found in stage3]
    dys = [grad_out[s * length : (s + 1) * length] for s in across]
    normed3 = [found[3] for found in stage3]
    grad_w_out = weight_part(index, dys, [found[4] for found in stage3], second_order, "grad_ffn_out")
    dgus = [found[5] for found in stage3]
    grad_gate = weight_part(index, normed3, [d[:, :units] for d in dgus], first_order, "grad_gate")
    grad_up = weight_part(index, normed3, [d[:, units:] for d in dgus], third_order, "grad_up")
    mixed = jnp.concatenate(
        [(found[0] + swap(found[1])).astype(BF16) for found in stage3], axis=0
    )
    back_scratch = [
        pltpu.VMEM((length, width), BF16), pltpu.VMEM((width, length), BF16), pltpu.VMEM((width, length), BF16),
        pltpu.VMEM((width, length), F32), pltpu.VMEM((width, length), F32),
    ]
    stage4 = []
    for s in across:
        stage4.append(call(
            functools.partial(cross_backward, width=width), "cross_backward",
            [shape((length, model), F32), shape((length, model), F32), shape((length, model), BF16),
             shape((length, 3 * width), BF16), shape((encoded, half), F32), shape((encoded, half), F32),
             shape((1, model), F32)],
            [side, rows(grad_out, s), stage3[s][6], swapped3[s], stage3[s][2], gains[2], stage2[s][3],
             encoded_kv[s], stage2[s][5], cross_q, kv2, cross_o],
            scratch=back_scratch + [pltpu.VMEM((encoded, model), F32)],
            smem=1, flops=8 * length * model * width + 5 * scores // 2, spent=length * length * heads,
        ))
    swapped4 = [swap(found[0]) for found in stage4]
    grad_memory = jnp.stack([found[4] + swap(found[5]) for found in stage4], axis=0)
    grad_cross_kv = weight_part(
        index, [encoder[s * encoded : (s + 1) * encoded] for s in across],
        [found[3][:, width:] for found in stage4], second_order, "grad_cross_kv")
    grad_cross_o = weight_part(
        index, [found[2] for found in stage4], [found[4] for found in stage2], first_order, "grad_cross_o")
    grad_cross_q = weight_part(
        index, [found[2] for found in stage2], [found[3][:, :width] for found in stage4], first_order,
        "grad_cross_q")
    stage5 = []
    for s in across:
        stage5.append(call(
            functools.partial(self_backward, seq=s, width=width), "self_backward",
            [shape((length, model), F32), shape((length, model), F32), shape((length, model), BF16),
             shape((length, 3 * width), BF16), shape((heads, length, length), BF16), shape((1, model), F32)],
            [seq_len, stage4[s][1], stage4[s][0], swapped4[s], stage2[s][1], gains[1], stage1[s][2],
             stage1[s][4], self_q, kv1, self_o, table, rel_bucket],
            scratch=back_scratch,
            smem=1, flops=8 * length * model * width + 5 * scores // 2, spent=length * length * heads,
        ))
    swapped5 = [swap(found[0]) for found in stage5]
    normed1 = [found[1] for found in stage1]
    grad_self_kv = weight_part(
        index, normed1, [found[3][:, width:] for found in stage5], second_order, "grad_self_kv")
    grad_self_o = weight_part(
        index, [found[2] for found in stage5], [found[3] for found in stage1], first_order, "grad_self_o")
    grad_self_q = weight_part(
        index, normed1, [found[3][:, :width] for found in stage5], first_order, "grad_self_q")
    spread = call(
        functools.partial(table_backward, buckets=buckets), "table_backward",
        [shape((heads * 8, 8 * buckets), F32)], [rel_bucket, stage5[0][4], stage5[1][4]],
        scratch=[pltpu.VMEM((heads * 8, 8 * buckets), F32)],
        flops=4 * heads * length * length * 8 * buckets,
    )[0]
    table_grad = spread.reshape(heads, 8, 8, buckets).sum(axis=(1, 2)).T
    stage6 = []
    for s in across:
        stage6.append(call(
            input_backward, "input_backward",
            [shape((length, model), F32), shape((1, model), F32)],
            [stage5[s][1], stage5[s][0], swapped5[s], rows(layer_in, s), gains[0]],
        ))
    grad_layer_in = jnp.concatenate([found[0] for found in stage6], axis=0)
    gain1 = sum(found[1] for found in stage6)
    gain2 = sum(found[5] for found in stage5)
    gain3 = sum(found[6] for found in stage4)
    small = dp_sum(jnp.concatenate([gain1[0], gain2[0], gain3[0], table_grad.reshape(-1)]))
    per = model // count
    begin = index[0] * per
    gain_grads = [lax.dynamic_slice_in_dim(small, i * model + begin, per, 0) for i in range(3)]
    grad_table = small[3 * model :].reshape(buckets, heads)
    return (
        mixed,
        grad_layer_in,
        grad_memory,
        *gain_grads,
        grad_table,
        grad_self_q,
        grad_self_kv.reshape(per, 2, width),
        grad_self_o.T,
        grad_cross_q,
        grad_cross_kv.reshape(per, 2, width),
        grad_cross_o.T,
        jnp.stack([grad_gate, grad_up], axis=1),
        grad_w_out.T,
    )


def solution(mesh):
    placed = (
        P("dp", None),
        P("dp", None, None),
        P("dp", None),
        P("dp"),
        P(),
        P(),
        P(),
        P(),
        P(None, "mp"),
        P(None, "mp"),
        P(None, None, "mp"),
        P("mp", None),
        P(None, "mp"),
        P(None, None, "mp"),
        P("mp", None),
        P(None, None, "mp"),
        P("mp", None),
    )
    return jax.shard_map(
        on_device,
        mesh=mesh,
        in_specs=placed,
        out_specs=(
            P("dp", "mp"),
            P("dp", None),
            P("dp", None, "mp"),
            P("dp"),
            P("dp"),
            P("dp"),
            P(None, "mp"),
            P("dp", "mp"),
            P("dp", None, "mp"),
            P("mp", "dp"),
            P("dp", "mp"),
            P("dp", None, "mp"),
            P("mp", "dp"),
            P("dp", None, "mp"),
            P("mp", "dp"),
        ),
        check_vma=False,
    )
```

```python
import functools

import jax
import jax.numpy as jnp
from jax import lax
from jax.experimental import pallas as pl
from jax.experimental.pallas import tpu as pltpu
from jax.sharding import PartitionSpec as P

EPS = 1e-06
NEGATIVE = -1e30
F32 = jnp.float32
BF16 = jnp.bfloat16
LANES = 128
QB = 128
LIMIT = 26 * 2**20


def nn(left, right):
    return lax.dot_general(left, right, (((1,), (0,)), ((), ())), preferred_element_type=F32)


def nt(left, right):
    return lax.dot_general(left, right, (((1,), (1,)), ((), ())), preferred_element_type=F32)


def norm(values, gain):
    inverse = lax.rsqrt(jnp.mean(values * values, axis=-1, keepdims=True) + EPS)
    scaled = values * inverse
    return scaled * gain, scaled, inverse


def norm_back(grad, values, gain):
    inverse = lax.rsqrt(jnp.mean(values * values, axis=-1, keepdims=True) + EPS)
    scaled = values * inverse
    grad_scaled = grad * gain
    inner = jnp.mean(grad_scaled * scaled, axis=-1, keepdims=True)
    gain_grad = jnp.sum(grad * scaled, axis=0, keepdims=True)
    return inverse * (grad_scaled - scaled * inner), gain_grad


def own_half(value, side):
    lane = lax.broadcasted_iota(jnp.int32, value.shape, 1)
    keep = lane < LANES // 2 if side == 0 else lane >= LANES // 2
    return jnp.where(keep, value, jnp.zeros_like(value))


def join_halves(first, second):
    lane = lax.broadcasted_iota(jnp.int32, first.shape, 1)
    return jnp.where(lane < LANES // 2, first, second)


def bias_of(table_ref, bucket_ref, head, start, rows, keys):
    row = jnp.broadcast_to(table_ref[pl.ds(head, 1), :], (rows, LANES))
    parts = []
    for first in range(0, keys, LANES):
        index = bucket_ref[start : start + rows, first : first + LANES]
        parts.append(jnp.take_along_axis(row, index, axis=1, mode="promise_in_bounds"))
    return jnp.concatenate(parts, axis=1) if len(parts) > 1 else parts[0]


def masked(raw, start, count):
    rows, keys = raw.shape
    place = lax.broadcasted_iota(jnp.int32, (rows, 1), 0) + (start + 1)
    limit = jnp.minimum(place, count)
    column = lax.broadcasted_iota(jnp.int32, raw.shape, 1)
    return jnp.where(column < limit, raw, NEGATIVE)


def attend(q_ref, k_ref, v_ref, c_ref, lse_ref, length, keys_all, score):
    pairs = q_ref.shape[1] // LANES
    lane = lax.broadcasted_iota(jnp.int32, (QB, LANES), 1)

    def one_pair(pair, carry):
        columns = pl.ds(pl.multiple_of(pair * LANES, LANES), LANES)
        for start in range(0, length, QB):
            keys = keys_all(start)
            query = q_ref[start : start + QB, columns]
            key = k_ref[0:keys, columns]
            value = v_ref[0:keys, columns]
            found = []
            kept = lse_ref[start : start + QB, :]
            for side in range(2):
                head = pair * 2 + side
                raw = score(nt(own_half(query, side), key), head, start)
                top = jnp.max(raw, axis=1, keepdims=True)
                weight = jnp.exp(raw - top)
                total = jnp.sum(weight, axis=1, keepdims=True)
                probs = (weight * (1.0 / total)).astype(BF16)
                found.append(nn(probs, value))
                kept = jnp.where(lane == head, top + jnp.log(total), kept)
            lse_ref[start : start + QB, :] = kept
            c_ref[start : start + QB, columns] = join_halves(*found).astype(BF16)
        return carry

    lse_ref[...] = jnp.zeros_like(lse_ref)
    lax.fori_loop(0, pairs, one_pair, 0)


def attend_back(q_ref, k_ref, v_ref, dc_ref, lse_ref, d_ref, qt, dct, dkt, dvt, ds_ref, length, keys_all, score):
    width = q_ref.shape[1]
    pairs = width // LANES
    lane = lax.broadcasted_iota(jnp.int32, (QB, LANES), 1)
    qt[...] = q_ref[...].T
    dct[...] = dc_ref[...].T
    half = LANES // 2

    def one_pair(pair, carry):
        columns = pl.ds(pl.multiple_of(pair * LANES, LANES), LANES)
        for start in range(0, length, QB):
            rows = slice(start, start + QB)
            keys = keys_all(start)
            query = q_ref[rows, columns]
            grad = dc_ref[rows, columns]
            key = k_ref[0:keys, columns]
            value = v_ref[0:keys, columns]
            lse_all = lse_ref[rows, :]
            found = []
            for side in range(2):
                head = pair * 2 + side
                lse = jnp.sum(jnp.where(lane == head, lse_all, 0.0), axis=1, keepdims=True)
                raw = score(nt(own_half(query, side), key), head, start)
                probs = jnp.exp(raw - lse)
                grad_probs = nt(own_half(grad, side), value)
                inner = jnp.sum(probs * grad_probs, axis=1, keepdims=True)
                low = probs.astype(BF16)
                grad_raw = (probs * (grad_probs - inner)).astype(BF16)
                if ds_ref is not None:
                    ds_ref[pl.ds(head, 1), rows, 0:keys] = grad_raw[None]
                found.append(nn(grad_raw, key))
                place = pl.ds(pl.multiple_of(pair * LANES + side * half, half), half)
                add_k = nn(qt[place, rows], grad_raw)
                add_v = nn(dct[place, rows], low)
                if start == 0:
                    dkt[place, 0:keys] = add_k
                    dvt[place, 0:keys] = add_v
                else:
                    before = keys_all(start - QB)
                    dkt[place, 0:before] += add_k[:, 0:before]
                    dvt[place, 0:before] += add_v[:, 0:before]
                    if before < keys:
                        dkt[place, before:keys] = add_k[:, before:keys]
                        dvt[place, before:keys] = add_v[:, before:keys]
            d_ref[rows, columns] = join_halves(*found).astype(BF16)
        return carry

    lax.fori_loop(0, pairs, one_pair, 0)
    d_ref[:, width : 2 * width] = dkt[...].astype(BF16).T
    d_ref[:, 2 * width : 3 * width] = dvt[...].astype(BF16).T


def causal_keys(start):
    return start + QB


def self_forward(len_ref, x_ref, gain_ref, wq_ref, wkv_ref, wo_ref, table_ref, bucket_ref,
                 part_ref, n_ref, qkv_ref, c_ref, lse_ref, *, seq, width):
    length = x_ref.shape[0]
    normed, _, _ = norm(x_ref[...].astype(F32), gain_ref[...])
    n_ref[...] = normed.astype(BF16)
    qkv_ref[:, 0:width] = nn(n_ref[...], wq_ref[...]).astype(BF16)
    qkv_ref[:, width:] = nn(n_ref[...], wkv_ref[...]).astype(BF16)
    count = len_ref[seq]

    def score(raw, head, start):
        biased = raw + bias_of(table_ref, bucket_ref, head, start, *raw.shape)
        return masked(biased, start, count)

    attend(qkv_ref.at[:, 0:width], qkv_ref.at[:, width : 2 * width], qkv_ref.at[:, 2 * width : 3 * width],
           c_ref, lse_ref, length, causal_keys, score)
    part_ref[...] = nn(c_ref[...], wo_ref[...])


def project(x_ref, w_ref, out_ref):
    out_ref[...] = nn(x_ref[...], w_ref[...]).astype(out_ref.dtype)


def cross_forward(x_ref, mine_ref, theirs_ref, gain_ref, wq_ref, wo_ref, kv_ref,
                  part_ref, h_ref, n_ref, q_ref, c_ref, lse_ref, *, width):
    hidden = x_ref[...].astype(F32) + (mine_ref[...] + theirs_ref[...])
    h_ref[...] = hidden
    normed, _, _ = norm(hidden, gain_ref[...])
    n_ref[...] = normed.astype(BF16)
    q_ref[...] = nn(n_ref[...], wq_ref[...]).astype(BF16)
    keys = kv_ref.shape[0]
    attend(q_ref, kv_ref.at[:, 0:width], kv_ref.at[:, width : 2 * width], c_ref, lse_ref,
           x_ref.shape[0], lambda start: keys, lambda raw, head, start: raw)
    part_ref[...] = nn(c_ref[...], wo_ref[...])


GELU_C = 0.7978845608028654
GELU_A = 0.044715


def ffn_both(side_ref, h_ref, mine_ref, theirs_ref, gain_ref, dy_ref, win_ref, wout_ref,
             mixed_ref, h2_ref, n_ref, inner_ref, dgu_ref, dn_ref, scratch):
    hidden = h_ref[...] + (mine_ref[...] + theirs_ref[...])
    h2_ref[...] = hidden
    normed, _, _ = norm(hidden, gain_ref[...])
    n_ref[...] = normed.astype(BF16)
    units = wout_ref.shape[0]
    step = 256

    def one(chunk, carry):
        first = pl.multiple_of(chunk * step, step)
        here = pl.ds(first, step)
        there = pl.ds(pl.multiple_of(units + chunk * step, step), step)
        gate = nn(n_ref[...], win_ref[:, here])
        upward = nn(n_ref[...], win_ref[:, there])
        grad = nt(dy_ref[...], wout_ref[here, :])
        squared = gate * gate
        bent = jnp.tanh(gate * (GELU_C + (GELU_C * GELU_A) * squared))
        half = 0.5 + 0.5 * bent
        soft = gate * half
        slope = half + (0.5 * gate) * (1.0 - bent * bent) * (GELU_C + (3 * GELU_C * GELU_A) * squared)
        inner_ref[:, here] = (soft * upward).astype(BF16)
        dgu_ref[:, here] = (grad * upward * slope).astype(BF16)
        dgu_ref[:, there] = (grad * soft).astype(BF16)
        return carry

    lax.fori_loop(0, units // step, one, 0)
    model = h_ref.shape[1]
    dn_ref[:, 0:model] = nt(dgu_ref[...], win_ref[...])
    share = nn(inner_ref[...], wout_ref[...])
    scratch[...] = share
    half = mixed_ref.shape[1]
    me = side_ref[0]
    mine = pl.ds(pl.multiple_of(me * half, LANES), half)
    other = pl.ds(pl.multiple_of((1 - me) * half, LANES), half)
    mixed_ref[...] = h2_ref[:, mine] + scratch[:, mine]
    dn_ref[:, model:] = scratch[:, other]


def cross_backward(side_ref, dy_ref, mine_ref, theirs_ref, h_ref, gain_ref, q_ref, kv_ref, lse_ref,
                   wq_ref, wkv_ref, wo_ref,
                   dn_ref, dh_ref, da_ref, d_ref, gm_ref, gain_out_ref,
                   dc, qt, dct, dkt, dvt, scratch, *, width):
    back, gain_grad = norm_back(mine_ref[...] + theirs_ref[...], h_ref[...], gain_ref[...])
    gain_out_ref[...] = gain_grad
    grad = dy_ref[...].astype(F32) + back
    dh_ref[...] = grad
    da_ref[...] = grad.astype(BF16)
    dc[...] = nt(da_ref[...], wo_ref[...]).astype(BF16)
    keys = kv_ref.shape[0]
    attend_back(q_ref, kv_ref.at[:, 0:width], kv_ref.at[:, width : 2 * width], dc, lse_ref, d_ref,
                qt, dct, dkt, dvt, None, dy_ref.shape[0], lambda start: keys, lambda raw, head, start: raw)
    model = h_ref.shape[1]
    dn_ref[:, 0:model] = nt(d_ref[:, 0:width], wq_ref[...])
    scratch[...] = nt(d_ref[:, width : 3 * width], wkv_ref[...])
    half = gm_ref.shape[1]
    me = side_ref[0]
    gm_ref[...] = scratch[:, pl.ds(pl.multiple_of(me * half, LANES), half)]
    dn_ref[:, model:] = scratch[:, pl.ds(pl.multiple_of((1 - me) * half, LANES), half)]


def self_backward(len_ref, before_ref, mine_ref, theirs_ref, h_ref, gain_ref, qkv_ref, lse_ref,
                  wq_ref, wkv_ref, wo_ref, table_ref, bucket_ref,
                  dn_ref, dh_ref, da_ref, d_ref, ds_ref, gain_out_ref,
                  dc, qt, dct, dkt, dvt, *, seq, width):
    back, gain_grad = norm_back(mine_ref[...] + theirs_ref[...], h_ref[...], gain_ref[...])
    gain_out_ref[...] = gain_grad
    grad = before_ref[...] + back
    dh_ref[...] = grad
    da_ref[...] = grad.astype(BF16)
    dc[...] = nt(da_ref[...], wo_ref[...]).astype(BF16)
    count = len_ref[seq]

    def score(raw, head, start):
        biased = raw + bias_of(table_ref, bucket_ref, head, start, *raw.shape)
        return masked(biased, start, count)

    attend_back(qkv_ref.at[:, 0:width], qkv_ref.at[:, width : 2 * width], qkv_ref.at[:, 2 * width : 3 * width],
                dc, lse_ref, d_ref, qt, dct, dkt, dvt, ds_ref, h_ref.shape[0], causal_keys, score)
    dn_ref[...] = nt(d_ref[:, 0:width], wq_ref[...]) + nt(d_ref[:, width : 3 * width], wkv_ref[...])


def input_backward(before_ref, mine_ref, theirs_ref, x_ref, gain_ref, out_ref, gain_out_ref):
    back, gain_grad = norm_back(mine_ref[...] + theirs_ref[...], x_ref[...].astype(F32), gain_ref[...])
    gain_out_ref[...] = gain_grad
    out_ref[...] = before_ref[...] + back


def table_backward(_, bucket_ref, first_ref, second_ref, out_ref, total, *, buckets):
    heads, length, _ = first_ref.shape
    group = 8

    def one(block, carry, keys):
        start = pl.multiple_of(block * group, group)
        rows = pl.ds(start, group)
        code = bucket_ref[rows, 0:keys]
        spread = lax.broadcasted_iota(jnp.int32, (buckets, keys), 0)
        column = lax.broadcasted_iota(jnp.int32, (1, keys), 1)
        pieces = []
        for i in range(group):
            seen = jnp.where(column <= start + i, code[i : i + 1, :], -1)
            pieces.append((spread == seen).astype(F32))
        chosen = jnp.concatenate(pieces, axis=0).astype(BF16)
        both = []
        for ref in (first_ref, second_ref):
            values = ref[:, rows, 0:keys].astype(F32)
            both.append(values.reshape(heads * group, keys))
        total[...] += nt(jnp.concatenate(both, axis=0).astype(BF16), chosen)
        return carry

    total[...] = jnp.zeros_like(total)
    for start in range(0, length, QB):
        lax.fori_loop(start // group, (start + QB) // group, functools.partial(one, keys=start + QB), 0)
    row = lax.broadcasted_iota(jnp.int32, total.shape, 0)
    column = lax.broadcasted_iota(jnp.int32, total.shape, 1)
    out_ref[...] = jnp.where(lax.rem(row, group) == column // buckets, total[...], 0.0)


def weight_grad(index_ref, l0_ref, l1_ref, r0_ref, r1_ref, *rest, stride, blocks):
    outs, (turned, scratch) = rest[:-2], rest[-2:]
    length = l0_ref.shape[0]

    @pl.when(pl.program_id(0) == 0)
    def _():
        turned[:, 0:length] = l0_ref[...].T
        turned[:, length : 2 * length] = l1_ref[...].T

    value = nn(turned[:, 0:length], r0_ref[...]) + nn(turned[:, length : 2 * length], r1_ref[...])
    if stride is None:
        outs[0][...] = value
        return
    scratch[...] = value
    keep_ref, send_ref = outs
    block = scratch.shape[0] // blocks
    bit = lax.rem(index_ref[0] // stride, 2)
    for place in range(blocks // 2):
        low, high = place % stride, place // stride
        base = high * 2 * stride + low
        mine = pl.multiple_of((base + bit * stride) * block, 8)
        other = pl.multiple_of((base + (1 - bit) * stride) * block, 8)
        keep_ref[0, place] = scratch[pl.ds(mine, block), :]
        send_ref[0, place] = scratch[pl.ds(other, block), :]


def attention_grads(index_ref, *refs, strides, blocks, same):
    a0, a1, b0, b1, c0, c1, d0, d1, e0, e1 = refs[:10]
    outs, (turned, other, scratch) = refs[10:-3], refs[-3:]
    length, width = d0.shape
    step = pl.program_id(0)

    def turn(target, first, second):
        target[:, 0:length] = first[...].T
        target[:, length : 2 * length] = second[...].T

    @pl.when(step == 0)
    def _():
        turn(turned, a0, a1)
        turn(other, c0, c1)

    if not same:
        @pl.when(step == 1)
        def _():
            turn(turned, b0, b1)

    near, far = slice(0, length), slice(length, 2 * length)
    target = scratch if strides is not None else outs[0]
    target[:, 0:width] = nn(turned[:, near], d0[...]) + nn(turned[:, far], d1[...])
    target[:, width:] = nn(other[:, near], e0[...]) + nn(other[:, far], e1[...])
    if strides is None:
        return
    keep_ref, sends = outs[0], outs[1:]
    block = scratch.shape[0] // blocks
    for part, stride in enumerate(strides):
        @pl.when(step == part)
        def _(part=part, stride=stride):
            bit = lax.rem(index_ref[0] // stride, 2)
            for place in range(blocks // 2):
                low, high = place % stride, place // stride
                base = high * 2 * stride + low
                mine = pl.multiple_of((base + bit * stride) * block, 8)
                theirs = pl.multiple_of((base + (1 - bit) * stride) * block, 8)
                keep_ref[0, place] = scratch[pl.ds(mine, block), :]
                sends[part][0, place] = scratch[pl.ds(theirs, block), :]


def call(body, name, outs, args, scratch=(), smem=0, keep=(), shared=None):
    in_specs, arrays = [], []
    for place, value in enumerate(args):
        if place < smem:
            in_specs.append(pl.BlockSpec(memory_space=pltpu.SMEM))
            arrays.append(value)
            continue
        array, size, block, columns = value, value.shape[0] if not isinstance(value, tuple) else 0, 0, None
        if isinstance(value, tuple):
            array, size, block = value[:3]
            columns = value[3] if len(value) > 3 else None
        dims = (size,) + array.shape[1:] if columns is None else (size, columns)
        where = (block,) + (0,) * (array.ndim - 1)
        in_specs.append(pl.BlockSpec(dims, lambda i, where=where: where, pipeline_mode=pl.Buffered(1)))
        arrays.append(array)
    shapes, out_specs, aliases = [], [], {}
    for place, out in enumerate(outs):
        dims, where = out.shape, (0,) * len(out.shape)
        if shared is not None and place == shared[0]:
            where = (shared[1],) + where[1:]
            out = shape((shared[3] * dims[0],) + dims[1:], out.dtype)
        out_specs.append(pl.BlockSpec(dims, lambda i, where=where: where, pipeline_mode=pl.Buffered(1)))
        shapes.append(pltpu.HBM(out.shape, out.dtype) if place in keep else out)
    used = len(arrays)
    if shared is not None and shared[2] is not None:
        aliases[used] = shared[0]
        in_specs.append(pl.BlockSpec(memory_space=pl.ANY))
        arrays.append(shared[2])
    extra = len(arrays) - used

    def run(*refs):
        body(*refs[:used], *refs[used + extra :])

    return pl.pallas_call(
        run,
        name=name,
        grid=(1,),
        out_shape=shapes,
        in_specs=in_specs,
        out_specs=out_specs,
        scratch_shapes=list(scratch),
        input_output_aliases=aliases,
        compiler_params=pltpu.CompilerParams(vmem_limit_bytes=LIMIT),
    )(*arrays)


def shape(dims, dtype):
    return jax.ShapeDtypeStruct(dims, dtype)


def gate(value, *tokens):
    return lax.optimization_barrier((value,) + tokens)[0]


def swap(value):
    size = lax.axis_size("mp")
    return lax.ppermute(value, "mp", [(i, size - 1 - i) for i in range(size)])


def dp_swap(value, bit):
    return lax.ppermute(value, "dp", [(i, i ^ bit) for i in range(lax.axis_size("dp"))])


class Group:
    def __init__(self, index, block, columns):
        self.index, self.block, self.columns = index, block, columns
        self.count = lax.axis_size("dp")
        self.direct = block % 8 == 0 and self.count > 1
        self.round = 1
        self.parts = []
        self.tokens = []

    def left(self, order, rounds):
        return sorted(set(order) - set(order[:rounds]), reverse=True)

    def add(self, lefts, rights, order, name, after, first=0, columns=None):
        parts = [value if isinstance(value, tuple) else (value, 0) for value in lefts]
        lefts = [value for value, _ in parts]
        length, model = rights[0].shape[0], lefts[0].shape[1]
        columns = rights[0].shape[1] if columns is None else columns
        step = self.columns
        width = step if step % 512 else 512
        if self.direct:
            half = (columns // step, self.count // 2, self.block, step)
            outs = [pltpu.HBM(half, F32)] * 2
            per = step // width
            out_specs = [pl.BlockSpec((1,) + half[1:3] + (width,), lambda j: (j // per, 0, 0, j % per))] * 2
        else:
            outs = [shape((model, columns), F32)]
            out_specs = [pl.BlockSpec((model, width), lambda j: (0, j))]
        skip = first // width
        found = pl.pallas_call(
            functools.partial(weight_grad, stride=order[0] if self.direct else None, blocks=self.count),
            name=name,
            grid=(columns // width,),
            out_shape=outs,
            in_specs=[pl.BlockSpec(memory_space=pltpu.SMEM)]
            + [pl.BlockSpec((length, model), lambda j, place=place: (place, 0)) for _, place in parts]
            + [pl.BlockSpec((length, width), lambda j: (0, j + skip))] * 2,
            out_specs=out_specs,
            scratch_shapes=[pltpu.VMEM((model, 2 * length), BF16), pltpu.VMEM((model, width), F32)],
            compiler_params=pltpu.CompilerParams(vmem_limit_bytes=LIMIT),
        )(gate(self.index, *after), *lefts, *rights)
        if not self.direct:
            for start in range(0, columns, step):
                self.parts.append((order, found[0][:, start : start + step]))
            return [found[0]]
        keep, send = found
        arrived = self.exchange(send, order[0])
        for place in range(columns // step):
            self.parts.append((order, [(keep, place, 1), (arrived, place, 1)]))
        return [send]

    def add_attention(self, normed, keyed, grads, d, c, name, after):
        arrays = [value for pair in (normed, keyed, grads) for value, _ in pair]
        places = [place for pair in (normed, keyed, grads) for _, place in pair]
        length, width = c[0].shape
        model, third = arrays[0].shape[1], width // 3
        columns = self.columns
        orders = ring_orders(self.count)
        half = (1, self.count // 2, self.block, columns)
        fixed = lambda j: (0, 0, 0, 0)
        if self.direct:
            outs = [pltpu.HBM((3,) + half[1:], F32)] + [pltpu.HBM(half, F32)] * 3
            out_specs = [pl.BlockSpec(half, lambda j: (j, 0, 0, 0))] + [pl.BlockSpec(half, fixed)] * 3
        else:
            outs = [shape((model, 3 * columns), F32)]
            out_specs = [pl.BlockSpec((model, columns), lambda j: (0, j))]
        found = pl.pallas_call(
            functools.partial(
                attention_grads, strides=[order[0] for order in orders] if self.direct else None,
                blocks=self.count, same=normed is keyed),
            name=name,
            grid=(3,),
            out_shape=outs,
            in_specs=[pl.BlockSpec(memory_space=pltpu.SMEM)]
            + [pl.BlockSpec((length, model), lambda j, place=place: (place, 0)) for place in places]
            + [pl.BlockSpec((length, width), lambda j: (0, j))] * 2
            + [pl.BlockSpec((length, third), lambda j: (0, j))] * 2,
            out_specs=out_specs,
            scratch_shapes=[pltpu.VMEM((model, 2 * length), BF16)] * 2 + [pltpu.VMEM((model, columns), F32)],
            compiler_params=pltpu.CompilerParams(vmem_limit_bytes=40 * 2**20),
        )(gate(self.index, *after), *arrays, *d, *c)
        if not self.direct:
            for part, order in enumerate(orders):
                self.parts.append((order, found[0][:, part * columns : (part + 1) * columns]))
            return [found[0]], lambda *tokens: None

        def launch(*tokens):
            sends = lax.optimization_barrier((tuple(found[1:]), tokens))[0]
            for part, order in enumerate(orders):
                arrived = self.exchange(sends[part], order[0])
                self.parts.append((order, [(found[0], part, 1), (arrived, 0, 1)]))

        return list(found[1:]), launch

    def arrivals(self):
        if not self.direct:
            return []
        found = []
        for _, pieces in self.parts:
            if not any(pieces[-1][0] is value for value in found):
                found.append(pieces[-1][0])
        return found

    def exchange(self, value, stride):
        return lax.ppermute(value, "dp", [(i, i ^ stride) for i in range(self.count)])

    def advance(self, rounds, streams, other, tokens, name):
        arrays, specs, plan = [], [], []
        block, columns = self.block, self.columns
        blocks = 2 ** len(self.left(self.parts[0][0], rounds))
        for stream in streams:
            lengths = []
            for part in stream:
                order, pieces = self.parts[part]
                lengths.append(len(pieces))
                after = self.left(order, rounds)
                for value, place, since in pieces:
                    before = self.left(order, since)

                    def where(g, index, order=order, before=before, after=after, place=place):
                        bit = lambda value, at: lax.bitwise_and(lax.shift_right_logical(value, at), 1)
                        number = 0
                        for stride in before:
                            if stride in after:
                                chosen = bit(g, len(after) - 1 - after.index(stride))
                            else:
                                chosen = bit(index[0], stride.bit_length() - 1)
                                if other and stride == order[rounds - 1]:
                                    chosen = 1 - chosen
                            number = number * 2 + chosen
                        return place, number, 0, 0

                    arrays.append(value)
                    specs.append(pl.BlockSpec((1, 1, block, columns), where))
            plan.append(lengths)
        fresh = [i for i, value in enumerate(arrays) if any(value is p[-1][0] for _, p in self.parts)]
        gated = lax.optimization_barrier((self.index, tuple(arrays[i] for i in fresh), tuple(tokens)))
        for i, value in zip(fresh, gated[1]):
            arrays[i] = value
        arrays = [pltpu.with_memory_space_constraint(value, pltpu.HBM) for value in arrays]

        def body(_, *refs):
            refs = list(refs)
            for out, lengths in zip(refs[len(arrays):], plan):
                for place, amount in enumerate(lengths):
                    values = [refs.pop(0)[0, 0] for _ in range(amount)]
                    out[place, 0] = sum(values[1:], values[0])

        outs = [shape((len(stream), blocks, block, columns), F32) for stream in streams]
        return pl.pallas_call(
            body,
            name=name,
            grid_spec=pltpu.PrefetchScalarGridSpec(
                num_scalar_prefetch=1,
                grid=(blocks,),
                in_specs=specs,
                out_specs=[pl.BlockSpec((len(s), 1, block, columns), lambda g, _: (0, g, 0, 0)) for s in streams],
            ),
            out_shape=outs,
            compiler_params=pltpu.CompilerParams(vmem_limit_bytes=LIMIT),
        )(gated[0], *arrays)

    def step(self, *tokens):
        if not self.direct or self.round == len(self.parts[0][0]):
            return []
        self.round += 1
        strides = []
        for order, _ in self.parts:
            if order[self.round - 1] not in strides:
                strides.append(order[self.round - 1])
        streams = [[i for i, (order, _) in enumerate(self.parts) if order[self.round - 1] == stride]
                   for stride in strides]
        sends = self.advance(self.round, streams, True, tokens, "advance%d" % self.round)
        for stride, stream, send in zip(strides, streams, sends):
            arrived = self.exchange(send, stride)
            for place, part in enumerate(stream):
                self.parts[part][1].append((arrived, place, self.round))
        return list(sends)

    def finish(self, *tokens):
        if not self.direct:
            return [lax.psum_scatter(whole, "dp", scatter_dimension=0, tiled=True) for _, whole in self.parts]
        while self.round < len(self.parts[0][0]):
            self.step(*tokens)
        found = self.advance(self.round, [[i] for i in range(len(self.parts))], False, tokens, "settle")
        return [value.reshape(self.block, self.columns) for value in found]


def orders(count):
    bits = []
    bit = 1
    while bit < count:
        bits.append(bit)
        bit *= 2
    if len(bits) != 4:
        return bits, bits, bits
    return [1, 2, 4, 8], [2, 1, 4, 8], [4, 1, 2, 8]


def ring_orders(count):
    found = orders(count)
    return ([1, 2, 4, 8], [2, 4, 1, 8], [4, 1, 2, 8]) if count == 16 else found


def on_device(
    layer_in,
    memory,
    grad_out,
    seq_len,
    rel_bucket,
    self_gain,
    cross_gain,
    ffn_gain,
    rel_table,
    self_q,
    self_kv,
    self_o,
    cross_q,
    cross_kv,
    cross_o,
    ffn_in,
    ffn_out,
):
    buckets, heads = rel_table.shape
    width = self_q.shape[1]
    length = rel_bucket.shape[0]
    encoded = memory.shape[1]
    model = layer_in.shape[1]
    units = ffn_out.shape[0]
    seqs = seq_len.shape[0]
    half = model // lax.axis_size("mp")
    count = lax.axis_size("dp")
    side = lax.axis_index("mp").astype(jnp.int32).reshape(1)
    index = lax.axis_index("dp").astype(jnp.int32).reshape(1)
    table = jnp.zeros((8, LANES), F32).at[:heads, :buckets].set(rel_table.T)
    kv1 = self_kv.reshape(model, 2 * width)
    kv2 = cross_kv.reshape(model, 2 * width)
    w_in = ffn_in.reshape(model, 2 * units)
    gains = [g.reshape(1, model) for g in (self_gain, cross_gain, ffn_gain)]
    encoder = memory.reshape(seqs * encoded, model)
    across = range(seqs)
    rows = lambda array, s: (array, length, s)
    per = model // count
    ring = ring_orders(count)
    stage1 = []
    for s in across:
        stage1.append(call(
            functools.partial(self_forward, seq=s, width=width), "self_forward",
            [shape((length, model), F32), shape((length, model), BF16), shape((length, 3 * width), BF16),
             shape((length, width), BF16), shape((length, LANES), F32)],
            [seq_len, rows(layer_in, s), gains[0], self_q, kv1, self_o, table, rel_bucket],
            smem=1, keep=(1, 2, 3, 4),
        ))
    swapped1 = [swap(found[0]) for found in stage1]
    encoded_kv = [
        call(project, "encoder_kv", [shape((encoded, 2 * width), BF16)], [rows(encoder, s), kv2])[0]
        for s in across
    ]
    stage2 = []
    for s in across:
        stage2.append(call(
            functools.partial(cross_forward, width=width), "cross_forward",
            [shape((length, model), F32), shape((length, model), F32), shape((length, model), BF16),
             shape((length, width), BF16), shape((length, width), BF16), shape((length, LANES), F32)],
            [rows(layer_in, s), stage1[s][0], swapped1[s], gains[1], cross_q, cross_o, encoded_kv[s]],
            keep=(2, 3, 4, 5),
        ))
    swapped2 = [swap(found[0]) for found in stage2]
    stage3, joint = [], None
    for s in across:
        stage3.append(call(
            ffn_both, "ffn_both",
            [shape((length, half), F32), shape((length, model), F32),
             shape((length, model), BF16), shape((length, units), BF16), shape((length, 2 * units), BF16),
             shape((length, model + half), F32)],
            [side, stage2[s][1], stage2[s][0], swapped2[s], gains[2], rows(grad_out, s), w_in, ffn_out],
            scratch=[pltpu.VMEM((length, model), F32)],
            smem=1, keep=(0,), shared=(5, s, joint, seqs),
        ))
        joint = stage3[s][5]
    swapped3 = swap(joint)
    grad3 = joint
    normed3 = [found[2] for found in stage3]
    dgus = [found[4] for found in stage3]
    ffn = Group(index, per, units)
    after = ffn.add(
        [(grad_out, s) for s in across], [found[3] for found in stage3], ring[1], "grad_ffn_out", [joint])
    after = ffn.add(normed3, dgus, ring[0], "grad_gate", after, 0, units)
    after = ffn.add(normed3, dgus, ring[2], "grad_up", after, units, units)
    back_scratch = [
        pltpu.VMEM((length, width), BF16), pltpu.VMEM((width, length), BF16), pltpu.VMEM((width, length), BF16),
        pltpu.VMEM((width, length), F32), pltpu.VMEM((width, length), F32),
    ]
    stage4, joint = [], None
    for s in across:
        stage4.append(call(
            functools.partial(cross_backward, width=width), "cross_backward",
            [shape((length, model + half), F32), shape((length, model), F32), shape((length, model), BF16),
             shape((length, 3 * width), BF16), shape((encoded, half), F32), shape((1, model), F32)],
            [gate(side, *after), rows(grad_out, s), (grad3, length, s, model), (swapped3, length, s, model),
             stage3[s][1], gains[2], stage2[s][3], encoded_kv[s], stage2[s][5], cross_q, kv2, cross_o],
            scratch=back_scratch + [pltpu.VMEM((encoded, model), F32)],
            smem=1, keep=(4,), shared=(0, s, joint, seqs),
        ))
        joint = stage4[s][0]
        after = [stage4[s][5]]
    grad4 = joint
    swapped4 = swap(gate(grad4, *ffn.arrivals()))
    after = ffn.step(*after)
    pair = lambda found: [(value, 0) for value in found]
    both = Group(index, per, width + width // 3)
    after, launch = both.add_attention(
        pair([found[2] for found in stage2]), [(encoder, s) for s in across], pair([found[2] for found in stage4]),
        [found[3] for found in stage4], [found[4] for found in stage2], "grad_cross", after)
    stage5, joint = [], None
    for s in across:
        stage5.append(call(
            functools.partial(self_backward, seq=s, width=width), "self_backward",
            [shape((length, model), F32), shape((length, model), F32), shape((length, model), BF16),
             shape((length, 3 * width), BF16), shape((heads, length, length), BF16), shape((1, model), F32)],
            [gate(seq_len, *after), stage4[s][1], (grad4, length, s, model), (swapped4, length, s, model),
             stage2[s][1], gains[1], stage1[s][2], stage1[s][4], self_q, kv1, self_o, table, rel_bucket],
            scratch=back_scratch,
            smem=1, shared=(0, s, joint, seqs),
        ))
        joint = stage5[s][0]
        after = [stage5[s][5]]
        if s == 0:
            launch(*after, *ffn.arrivals())
    grad5 = joint
    swapped5 = swap(gate(grad5, *both.arrivals()))
    after = ffn.step(*after, *both.arrivals())
    normed1 = pair([found[1] for found in stage1])
    after, launch = both.add_attention(
        normed1, normed1, pair([found[2] for found in stage5]),
        [found[3] for found in stage5], [found[3] for found in stage1], "grad_self", after)
    launch(swapped5, *ffn.arrivals())
    after = ffn.step(swapped5, *after)
    stage6, joint = [], None
    for s in across:
        stage6.append(call(
            input_backward, "input_backward",
            [shape((length, model), F32), shape((1, model), F32)],
            [stage5[s][1], rows(grad5, s), rows(swapped5, s), rows(layer_in, s), gate(gains[0], *after)],
            keep=(0,), shared=(0, s, joint, seqs),
        ))
        joint = stage6[s][0]
        after = [stage6[s][1]]
    grad_layer_in = joint
    spread = call(
        functools.partial(table_backward, buckets=buckets), "table_backward",
        [shape((2 * heads * 8, 8 * buckets), F32)],
        [gate(index, *after), rel_bucket, stage5[0][4], stage5[1][4]],
        scratch=[pltpu.VMEM((2 * heads * 8, 8 * buckets), F32)], smem=1,
    )[0]
    table_grad = spread.reshape(2, heads, 8, 8, buckets).sum(axis=(0, 2, 3)).T
    after = both.step(spread, *ffn.arrivals())
    grad_w_out, grad_gate, grad_up = ffn.finish(spread, *after)
    theirs3, theirs4 = gate(swapped3, spread, *after), gate(swapped4, spread, *after)
    mixed = jnp.concatenate([found[0] for found in stage3], axis=0)
    mixed = (mixed + theirs3[:, model:]).astype(BF16)
    grad_memory = jnp.concatenate([found[4] for found in stage4], axis=0) + theirs4[:, model:]
    grad_memory = grad_memory.reshape(seqs, encoded, half)
    gain1 = sum(found[1] for found in stage6)
    gain2 = sum(found[5] for found in stage5)
    gain3 = sum(found[5] for found in stage4)
    small = jnp.concatenate([gain1[0], gain2[0], gain3[0], table_grad.reshape(-1)])
    bits = sorted(orders(count)[0], reverse=True)
    arrived = dp_swap(small, bits[0])
    for bit in bits[1:-2]:
        after = both.step(*both.arrivals(), arrived)
        small = small + gate(arrived, *after)
        arrived = dp_swap(small, bit)
    after = both.step(*both.arrivals(), arrived)
    small = small + gate(arrived, *after)
    for bit in bits[-2:]:
        small = small + dp_swap(small, bit)
    settled = both.finish()
    results = []
    for first in (0, 3):
        q, k, v = [value[:, :width] for value in settled[first : first + 3]]
        o = jnp.concatenate([value[:, width:] for value in settled[first : first + 3]], axis=1)
        results.append((q, jnp.stack([k, v], axis=1), o))
    (grad_cross_q, grad_cross_kv, grad_cross_o), (grad_self_q, grad_self_kv, grad_self_o) = results
    begin = index[0] * per
    gain_grads = [lax.dynamic_slice_in_dim(small, i * model + begin, per, 0) for i in range(3)]
    grad_table = small[3 * model :].reshape(buckets, heads)
    return (
        mixed,
        grad_layer_in,
        grad_memory,
        *gain_grads,
        grad_table,
        grad_self_q,
        grad_self_kv,
        grad_self_o.T,
        grad_cross_q,
        grad_cross_kv,
        grad_cross_o.T,
        jnp.stack([grad_gate, grad_up], axis=1),
        grad_w_out.T,
    )


def solution(mesh):
    placed = (
        P("dp", None),
        P("dp", None, None),
        P("dp", None),
        P("dp"),
        P(),
        P(),
        P(),
        P(),
        P(None, "mp"),
        P(None, "mp"),
        P(None, None, "mp"),
        P("mp", None),
        P(None, "mp"),
        P(None, None, "mp"),
        P("mp", None),
        P(None, None, "mp"),
        P("mp", None),
    )
    return jax.shard_map(
        on_device,
        mesh=mesh,
        in_specs=placed,
        out_specs=(
            P("dp", "mp"),
            P("dp", None),
            P("dp", None, "mp"),
            P("dp"),
            P("dp"),
            P("dp"),
            P(None, "mp"),
            P("dp", "mp"),
            P("dp", None, "mp"),
            P("mp", "dp"),
            P("dp", "mp"),
            P("dp", None, "mp"),
            P("mp", "dp"),
            P("dp", None, "mp"),
            P("mp", "dp"),
        ),
        check_vma=False,
    )
```

```python
import functools

import jax
import jax.numpy as jnp
from jax import lax
from jax.experimental import pallas as pl
from jax.experimental.pallas import tpu as pltpu
from jax.sharding import PartitionSpec as P

EPS = 1e-06
NEGATIVE = -1e30
F32 = jnp.float32
BF16 = jnp.bfloat16
LANES = 128
QB = 256
TB = 128
QC = 512
LIMIT = 26 * 2**20


def nn(left, right):
    return lax.dot_general(left, right, (((1,), (0,)), ((), ())), preferred_element_type=F32)


def nt(left, right):
    return lax.dot_general(left, right, (((1,), (1,)), ((), ())), preferred_element_type=F32)


def norm(values, gain):
    inverse = lax.rsqrt(jnp.mean(values * values, axis=-1, keepdims=True) + EPS)
    scaled = values * inverse
    return scaled * gain, scaled, inverse


def norm_back(grad, values, gain):
    inverse = lax.rsqrt(jnp.mean(values * values, axis=-1, keepdims=True) + EPS)
    scaled = values * inverse
    grad_scaled = grad * gain
    inner = jnp.mean(grad_scaled * scaled, axis=-1, keepdims=True)
    gain_grad = jnp.sum(grad * scaled, axis=0, keepdims=True)
    return inverse * (grad_scaled - scaled * inner), gain_grad


def own_half(value, side):
    lane = lax.broadcasted_iota(jnp.int32, value.shape, 1)
    keep = lane < LANES // 2 if side == 0 else lane >= LANES // 2
    return jnp.where(keep, value, jnp.zeros_like(value))


def join_halves(first, second):
    lane = lax.broadcasted_iota(jnp.int32, first.shape, 1)
    return jnp.where(lane < LANES // 2, first, second)


def bias_of(table_ref, bucket_ref, head, start, rows, keys):
    row = jnp.broadcast_to(table_ref[pl.ds(head, 1), :], (rows, LANES))
    parts = []
    for first in range(0, keys, LANES):
        index = bucket_ref[start : start + rows, first : first + LANES]
        parts.append(jnp.take_along_axis(row, index, axis=1, mode="promise_in_bounds"))
    return jnp.concatenate(parts, axis=1) if len(parts) > 1 else parts[0]


def masked(raw, start, count):
    rows, keys = raw.shape
    place = lax.broadcasted_iota(jnp.int32, (rows, 1), 0) + (start + 1)
    limit = jnp.minimum(place, count)
    column = lax.broadcasted_iota(jnp.int32, raw.shape, 1)
    return jnp.where(column < limit, raw, NEGATIVE)


def attend(q_ref, k_ref, v_ref, c_ref, lse_ref, length, keys_all, score, block=QB):
    pairs = q_ref.shape[1] // LANES
    lane = lax.broadcasted_iota(jnp.int32, (block, LANES), 1)

    def one_pair(pair, carry):
        columns = pl.ds(pl.multiple_of(pair * LANES, LANES), LANES)
        for start in range(0, length, block):
            keys = keys_all(start)
            query = q_ref[start : start + block, columns]
            key = k_ref[0:keys, columns]
            value = v_ref[0:keys, columns]
            found = []
            kept = lse_ref[start : start + block, :]
            for side in range(2):
                head = pair * 2 + side
                raw = score(nt(own_half(query, side), key), head, start)
                top = jnp.max(raw, axis=1, keepdims=True)
                weight = jnp.exp(raw - top)
                total = jnp.sum(weight, axis=1, keepdims=True)
                probs = (weight * (1.0 / total)).astype(BF16)
                found.append(nn(probs, value))
                kept = jnp.where(lane == head, top + jnp.log(total), kept)
            lse_ref[start : start + block, :] = kept
            c_ref[start : start + block, columns] = join_halves(*found).astype(BF16)
        return carry

    lse_ref[...] = jnp.zeros_like(lse_ref)
    lax.fori_loop(0, pairs, one_pair, 0)


def attend_back(q_ref, k_ref, v_ref, dc_ref, lse_ref, d_ref, qt, dct, dkt, dvt, ds_ref, length, keys_all, score, block=QB):
    width = q_ref.shape[1]
    pairs = width // LANES
    lane = lax.broadcasted_iota(jnp.int32, (block, LANES), 1)
    qt[...] = q_ref[...].T
    dct[...] = dc_ref[...].T
    half = LANES // 2

    def one_pair(pair, carry):
        columns = pl.ds(pl.multiple_of(pair * LANES, LANES), LANES)
        for start in range(0, length, block):
            rows = slice(start, start + block)
            keys = keys_all(start)
            query = q_ref[rows, columns]
            grad = dc_ref[rows, columns]
            key = k_ref[0:keys, columns]
            value = v_ref[0:keys, columns]
            lse_all = lse_ref[rows, :]
            found = []
            for side in range(2):
                head = pair * 2 + side
                lse = jnp.sum(jnp.where(lane == head, lse_all, 0.0), axis=1, keepdims=True)
                raw = score(nt(own_half(query, side), key), head, start)
                probs = jnp.exp(raw - lse)
                grad_probs = nt(own_half(grad, side), value)
                inner = jnp.sum(probs * grad_probs, axis=1, keepdims=True)
                low = probs.astype(BF16)
                grad_raw = (probs * (grad_probs - inner)).astype(BF16)
                if ds_ref is not None:
                    ds_ref[pl.ds(head, 1), rows, 0:keys] = grad_raw[None]
                found.append(nn(grad_raw, key))
                place = pl.ds(pl.multiple_of(pair * LANES + side * half, half), half)
                add_k = nn(qt[place, rows], grad_raw)
                add_v = nn(dct[place, rows], low)
                if start == 0:
                    dkt[place, 0:keys] = add_k
                    dvt[place, 0:keys] = add_v
                else:
                    before = keys_all(start - block)
                    dkt[place, 0:before] += add_k[:, 0:before]
                    dvt[place, 0:before] += add_v[:, 0:before]
                    if before < keys:
                        dkt[place, before:keys] = add_k[:, before:keys]
                        dvt[place, before:keys] = add_v[:, before:keys]
            d_ref[rows, columns] = join_halves(*found).astype(BF16)
        return carry

    lax.fori_loop(0, pairs, one_pair, 0)
    d_ref[:, width : 2 * width] = dkt[...].astype(BF16).T
    d_ref[:, 2 * width : 3 * width] = dvt[...].astype(BF16).T


def causal_keys(start):
    return start + QB


def self_forward(len_ref, x_ref, gain_ref, wq_ref, wkv_ref, wo_ref, table_ref, bucket_ref,
                 part_ref, n_ref, qkv_ref, c_ref, lse_ref, *, seq, width):
    length = x_ref.shape[0]
    normed, _, _ = norm(x_ref[...].astype(F32), gain_ref[...])
    n_ref[...] = normed.astype(BF16)
    qkv_ref[:, 0:width] = nn(n_ref[...], wq_ref[...]).astype(BF16)
    qkv_ref[:, width:] = nn(n_ref[...], wkv_ref[...]).astype(BF16)
    count = len_ref[seq]

    def score(raw, head, start):
        biased = raw + bias_of(table_ref, bucket_ref, head, start, *raw.shape)
        return masked(biased, start, count)

    attend(qkv_ref.at[:, 0:width], qkv_ref.at[:, width : 2 * width], qkv_ref.at[:, 2 * width : 3 * width],
           c_ref, lse_ref, length, causal_keys, score)
    part_ref[...] = nn(c_ref[...], wo_ref[...])


def project(x_ref, w_ref, out_ref):
    out_ref[...] = nn(x_ref[...], w_ref[...]).astype(out_ref.dtype)


def cross_forward(x_ref, mine_ref, theirs_ref, gain_ref, wq_ref, wo_ref, kv_ref,
                  part_ref, h_ref, n_ref, q_ref, c_ref, lse_ref, *, width):
    hidden = x_ref[...].astype(F32) + (mine_ref[...] + theirs_ref[...])
    h_ref[...] = hidden
    normed, _, _ = norm(hidden, gain_ref[...])
    n_ref[...] = normed.astype(BF16)
    q_ref[...] = nn(n_ref[...], wq_ref[...]).astype(BF16)
    keys = kv_ref.shape[0]
    attend(q_ref, kv_ref.at[:, 0:width], kv_ref.at[:, width : 2 * width], c_ref, lse_ref,
           x_ref.shape[0], lambda start: keys, lambda raw, head, start: raw, QC)
    part_ref[...] = nn(c_ref[...], wo_ref[...])


GELU_C = 0.7978845608028654
GELU_A = 0.044715


def ffn_both(side_ref, h_ref, mine_ref, theirs_ref, gain_ref, dy_ref, win_ref, wout_ref,
             mixed_ref, h2_ref, n_ref, inner_ref, dgu_ref, dn_ref, scratch):
    hidden = h_ref[...] + (mine_ref[...] + theirs_ref[...])
    h2_ref[...] = hidden
    normed, _, _ = norm(hidden, gain_ref[...])
    n_ref[...] = normed.astype(BF16)
    units = wout_ref.shape[0]
    step = 256

    def one(chunk, carry):
        first = pl.multiple_of(chunk * step, step)
        here = pl.ds(first, step)
        there = pl.ds(pl.multiple_of(units + chunk * step, step), step)
        gate = nn(n_ref[...], win_ref[:, here])
        upward = nn(n_ref[...], win_ref[:, there])
        grad = nt(dy_ref[...], wout_ref[here, :])
        squared = gate * gate
        bent = jnp.tanh(gate * (GELU_C + (GELU_C * GELU_A) * squared))
        half = 0.5 + 0.5 * bent
        soft = gate * half
        slope = half + (0.5 * gate) * (1.0 - bent * bent) * (GELU_C + (3 * GELU_C * GELU_A) * squared)
        inner_ref[:, here] = (soft * upward).astype(BF16)
        dgu_ref[:, here] = (grad * upward * slope).astype(BF16)
        dgu_ref[:, there] = (grad * soft).astype(BF16)
        return carry

    lax.fori_loop(0, units // step, one, 0)
    model = h_ref.shape[1]
    dn_ref[:, 0:model] = nt(dgu_ref[...], win_ref[...])
    share = nn(inner_ref[...], wout_ref[...])
    scratch[...] = share
    half = mixed_ref.shape[1]
    me = side_ref[0]
    mine = pl.ds(pl.multiple_of(me * half, LANES), half)
    other = pl.ds(pl.multiple_of((1 - me) * half, LANES), half)
    mixed_ref[...] = h2_ref[:, mine] + scratch[:, mine]
    dn_ref[:, model:] = scratch[:, other]


def cross_backward(side_ref, dy_ref, mine_ref, theirs_ref, h_ref, gain_ref, q_ref, kv_ref, lse_ref,
                   wq_ref, wkv_ref, wo_ref,
                   dn_ref, dh_ref, da_ref, d_ref, gm_ref, gain_out_ref, go_ref,
                   dc, qt, dct, dkt, dvt, scratch, *, width):
    back, gain_grad = norm_back(mine_ref[...] + theirs_ref[...], h_ref[...], gain_ref[...])
    gain_out_ref[...] = gain_grad
    grad = dy_ref[...].astype(F32) + back
    dh_ref[...] = grad
    da_ref[...] = grad.astype(BF16)
    dc[...] = nt(da_ref[...], wo_ref[...]).astype(BF16)
    keys = kv_ref.shape[0]
    attend_back(q_ref, kv_ref.at[:, 0:width], kv_ref.at[:, width : 2 * width], dc, lse_ref, d_ref,
                qt, dct, dkt, dvt, None, dy_ref.shape[0], lambda start: keys, lambda raw, head, start: raw, QC)
    dn_ref[...] = nt(d_ref[:, 0:width], wq_ref[...])
    scratch[...] = nt(d_ref[:, width : 3 * width], wkv_ref[...])
    half = gm_ref.shape[1]
    me = side_ref[0]
    gm_ref[...] = scratch[:, pl.ds(pl.multiple_of(me * half, LANES), half)]
    go_ref[...] = scratch[:, pl.ds(pl.multiple_of((1 - me) * half, LANES), half)]


def self_backward(len_ref, before_ref, mine_ref, theirs_ref, h_ref, gain_ref, qkv_ref, lse_ref,
                  wq_ref, wkv_ref, wo_ref, table_ref, bucket_ref,
                  dn_ref, dh_ref, da_ref, d_ref, ds_ref, gain_out_ref,
                  dc, qt, dct, dkt, dvt, *, seq, width):
    back, gain_grad = norm_back(mine_ref[...] + theirs_ref[...], h_ref[...], gain_ref[...])
    gain_out_ref[...] = gain_grad
    grad = before_ref[...] + back
    dh_ref[...] = grad
    da_ref[...] = grad.astype(BF16)
    dc[...] = nt(da_ref[...], wo_ref[...]).astype(BF16)
    count = len_ref[seq]

    def score(raw, head, start):
        biased = raw + bias_of(table_ref, bucket_ref, head, start, *raw.shape)
        return masked(biased, start, count)

    attend_back(qkv_ref.at[:, 0:width], qkv_ref.at[:, width : 2 * width], qkv_ref.at[:, 2 * width : 3 * width],
                dc, lse_ref, d_ref, qt, dct, dkt, dvt, ds_ref, h_ref.shape[0], causal_keys, score)
    dn_ref[...] = nt(d_ref[:, 0:width], wq_ref[...]) + nt(d_ref[:, width : 3 * width], wkv_ref[...])


def input_backward(before_ref, mine_ref, theirs_ref, x_ref, gain_ref, out_ref, gain_out_ref):
    back, gain_grad = norm_back(mine_ref[...] + theirs_ref[...], x_ref[...].astype(F32), gain_ref[...])
    gain_out_ref[...] = gain_grad
    out_ref[...] = before_ref[...] + back


def table_backward(_, bucket_ref, first_ref, second_ref, out_ref, total, *, buckets):
    heads, length, _ = first_ref.shape
    group = 8

    def one(block, carry, keys):
        start = pl.multiple_of(block * group, group)
        rows = pl.ds(start, group)
        code = bucket_ref[rows, 0:keys]
        spread = lax.broadcasted_iota(jnp.int32, (buckets, keys), 0)
        column = lax.broadcasted_iota(jnp.int32, (1, keys), 1)
        pieces = []
        for i in range(group):
            seen = jnp.where(column <= start + i, code[i : i + 1, :], -1)
            pieces.append((spread == seen).astype(F32))
        chosen = jnp.concatenate(pieces, axis=0).astype(BF16)
        both = []
        for ref in (first_ref, second_ref):
            values = ref[:, rows, 0:keys].astype(F32)
            both.append(values.reshape(heads * group, keys))
        total[...] += nt(jnp.concatenate(both, axis=0).astype(BF16), chosen)
        return carry

    total[...] = jnp.zeros_like(total)
    for start in range(0, length, TB):
        lax.fori_loop(start // group, (start + TB) // group, functools.partial(one, keys=start + TB), 0)
    row = lax.broadcasted_iota(jnp.int32, total.shape, 0)
    column = lax.broadcasted_iota(jnp.int32, total.shape, 1)
    out_ref[...] = jnp.where(lax.rem(row, group) == column // buckets, total[...], 0.0)


def weight_grad(index_ref, l0_ref, l1_ref, r0_ref, r1_ref, *rest, stride, blocks):
    outs, (turned, scratch) = rest[:-2], rest[-2:]
    length = l0_ref.shape[0]

    @pl.when(pl.program_id(0) == 0)
    def _():
        turned[:, 0:length] = l0_ref[...].T
        turned[:, length : 2 * length] = l1_ref[...].T

    value = nn(turned[:, 0:length], r0_ref[...]) + nn(turned[:, length : 2 * length], r1_ref[...])
    if stride is None:
        outs[0][...] = value
        return
    scratch[...] = value
    keep_ref, send_ref = outs
    block = scratch.shape[0] // blocks
    bit = lax.rem(index_ref[0] // stride, 2)
    for place in range(blocks // 2):
        low, high = place % stride, place // stride
        base = high * 2 * stride + low
        mine = pl.multiple_of((base + bit * stride) * block, 8)
        other = pl.multiple_of((base + (1 - bit) * stride) * block, 8)
        keep_ref[0, place] = scratch[pl.ds(mine, block), :]
        send_ref[0, place] = scratch[pl.ds(other, block), :]


def attention_grads(index_ref, *refs, strides, blocks, same):
    a0, a1, b0, b1, c0, c1, d0, d1, e0, e1 = refs[:10]
    outs, (turned, other, scratch) = refs[10:-3], refs[-3:]
    length, width = d0.shape
    step = pl.program_id(0)

    def turn(target, first, second):
        target[:, 0:length] = first[...].T
        target[:, length : 2 * length] = second[...].T

    @pl.when(step == 0)
    def _():
        turn(turned, a0, a1)
        turn(other, c0, c1)

    if not same:
        @pl.when(step == 1)
        def _():
            turn(turned, b0, b1)

    near, far = slice(0, length), slice(length, 2 * length)
    target = scratch if strides is not None else outs[0]
    target[:, 0:width] = nn(turned[:, near], d0[...]) + nn(turned[:, far], d1[...])
    target[:, width:] = nn(other[:, near], e0[...]) + nn(other[:, far], e1[...])
    if strides is None:
        return
    keep_ref, sends = outs[0], outs[1:]
    block = scratch.shape[0] // blocks
    for part, stride in enumerate(strides):
        @pl.when(step == part)
        def _(part=part, stride=stride):
            bit = lax.rem(index_ref[0] // stride, 2)
            for place in range(blocks // 2):
                low, high = place % stride, place // stride
                base = high * 2 * stride + low
                mine = pl.multiple_of((base + bit * stride) * block, 8)
                theirs = pl.multiple_of((base + (1 - bit) * stride) * block, 8)
                keep_ref[0, place] = scratch[pl.ds(mine, block), :]
                sends[part][0, place] = scratch[pl.ds(theirs, block), :]


def call(body, name, outs, args, scratch=(), smem=0, keep=(), shared=None, direct=False):
    in_specs, arrays = [], []
    for place, value in enumerate(args):
        if place < smem:
            in_specs.append(pl.BlockSpec(memory_space=pltpu.SMEM))
            arrays.append(value)
            continue
        array, size, block, columns = value, value.shape[0] if not isinstance(value, tuple) else 0, 0, None
        if isinstance(value, tuple):
            array, size, block = value[:3]
            columns = value[3] if len(value) > 3 else None
        dims = (size,) + array.shape[1:] if columns is None else (size, columns)
        where = (block,) + (0,) * (array.ndim - 1)
        in_specs.append(pl.BlockSpec(dims, lambda i, where=where: where, pipeline_mode=pl.Buffered(1)))
        arrays.append(array)
    shapes, out_specs, aliases = [], [], {}
    for place, out in enumerate(outs):
        dims, where = out.shape, (0,) * len(out.shape)
        if shared is not None and place == shared[0]:
            where = (shared[1],) + where[1:]
            out = shape((shared[3] * dims[0],) + dims[1:], out.dtype)
        out_specs.append(pl.BlockSpec(dims, lambda i, where=where: where, pipeline_mode=pl.Buffered(1)))
        shapes.append(pltpu.HBM(out.shape, out.dtype) if place in keep else out)
    used = len(arrays)
    if shared is not None and shared[2] is not None:
        aliases[used] = shared[0]
        in_specs.append(pl.BlockSpec(memory_space=pl.ANY))
        arrays.append(shared[2])
    extra = len(arrays) - used
    if direct:
        arrays[smem:used] = [pltpu.with_memory_space_constraint(a, pltpu.HBM) for a in arrays[smem:used]]

    def run(*refs):
        body(*refs[:used], *refs[used + extra :])

    return pl.pallas_call(
        run,
        name=name,
        grid=(1,),
        out_shape=shapes,
        in_specs=in_specs,
        out_specs=out_specs,
        scratch_shapes=list(scratch),
        input_output_aliases=aliases,
        compiler_params=pltpu.CompilerParams(vmem_limit_bytes=LIMIT),
    )(*arrays)


def shape(dims, dtype):
    return jax.ShapeDtypeStruct(dims, dtype)


def gate(value, *tokens):
    return lax.optimization_barrier((value,) + tokens)[0]


def swap(value):
    size = lax.axis_size("mp")
    return lax.ppermute(value, "mp", [(i, size - 1 - i) for i in range(size)])


def dp_swap(value, bit):
    return lax.ppermute(value, "dp", [(i, i ^ bit) for i in range(lax.axis_size("dp"))])


class Group:
    def __init__(self, index, block, columns):
        self.index, self.block, self.columns = index, block, columns
        self.count = lax.axis_size("dp")
        self.direct = block % 8 == 0 and self.count > 1
        self.round = 1
        self.parts = []
        self.tokens = []

    def left(self, order, rounds):
        return sorted(set(order) - set(order[:rounds]), reverse=True)

    def add(self, lefts, rights, order, name, after, first=0, columns=None):
        parts = [value if isinstance(value, tuple) else (value, 0) for value in lefts]
        lefts = [value for value, _ in parts]
        length, model = rights[0].shape[0], lefts[0].shape[1]
        columns = rights[0].shape[1] if columns is None else columns
        step = self.columns
        width = step if step % 512 else 512
        if self.direct:
            half = (columns // step, self.count // 2, self.block, step)
            outs = [pltpu.HBM(half, F32)] * 2
            per = step // width
            out_specs = [pl.BlockSpec((1,) + half[1:3] + (width,), lambda j: (j // per, 0, 0, j % per))] * 2
        else:
            outs = [shape((model, columns), F32)]
            out_specs = [pl.BlockSpec((model, width), lambda j: (0, j))]
        skip = first // width
        found = pl.pallas_call(
            functools.partial(weight_grad, stride=order[0] if self.direct else None, blocks=self.count),
            name=name,
            grid=(columns // width,),
            out_shape=outs,
            in_specs=[pl.BlockSpec(memory_space=pltpu.SMEM)]
            + [pl.BlockSpec((length, model), lambda j, place=place: (place, 0)) for _, place in parts]
            + [pl.BlockSpec((length, width), lambda j: (0, j + skip))] * 2,
            out_specs=out_specs,
            scratch_shapes=[pltpu.VMEM((model, 2 * length), BF16), pltpu.VMEM((model, width), F32)],
            compiler_params=pltpu.CompilerParams(vmem_limit_bytes=LIMIT),
        )(gate(self.index, *after), *lefts, *rights)
        if not self.direct:
            for start in range(0, columns, step):
                self.parts.append((order, found[0][:, start : start + step]))
            return [found[0]]
        keep, send = found
        arrived = self.exchange(send, order[0])
        for place in range(columns // step):
            self.parts.append((order, [(keep, place, 1), (arrived, place, 1)]))
        return [send]

    def add_attention(self, normed, keyed, grads, d, c, name, after):
        arrays = [value for pair in (normed, keyed, grads) for value, _ in pair]
        places = [place for pair in (normed, keyed, grads) for _, place in pair]
        length, width = c[0].shape
        model, third = arrays[0].shape[1], width // 3
        columns = self.columns
        orders = ring_orders(self.count)
        half = (1, self.count // 2, self.block, columns)
        fixed = lambda j: (0, 0, 0, 0)
        if self.direct:
            outs = [pltpu.HBM((3,) + half[1:], F32)] + [pltpu.HBM(half, F32)] * 3
            out_specs = [pl.BlockSpec(half, lambda j: (j, 0, 0, 0))] + [pl.BlockSpec(half, fixed)] * 3
        else:
            outs = [shape((model, 3 * columns), F32)]
            out_specs = [pl.BlockSpec((model, columns), lambda j: (0, j))]
        found = pl.pallas_call(
            functools.partial(
                attention_grads, strides=[order[0] for order in orders] if self.direct else None,
                blocks=self.count, same=normed is keyed),
            name=name,
            grid=(3,),
            out_shape=outs,
            in_specs=[pl.BlockSpec(memory_space=pltpu.SMEM)]
            + [pl.BlockSpec((length, model), lambda j, place=place: (place, 0)) for place in places]
            + [pl.BlockSpec((length, width), lambda j: (0, j))] * 2
            + [pl.BlockSpec((length, third), lambda j: (0, j))] * 2,
            out_specs=out_specs,
            scratch_shapes=[pltpu.VMEM((model, 2 * length), BF16)] * 2 + [pltpu.VMEM((model, columns), F32)],
            compiler_params=pltpu.CompilerParams(vmem_limit_bytes=40 * 2**20),
        )(gate(self.index, *after), *arrays, *d, *c)
        if not self.direct:
            for part, order in enumerate(orders):
                self.parts.append((order, found[0][:, part * columns : (part + 1) * columns]))
            return [found[0]], lambda *tokens: None

        def launch(*tokens):
            sends = lax.optimization_barrier((tuple(found[1:]), tokens))[0]
            for part, order in enumerate(orders):
                arrived = self.exchange(sends[part], order[0])
                self.parts.append((order, [(found[0], part, 1), (arrived, 0, 1)]))

        return list(found[1:]), launch

    def arrivals(self):
        if not self.direct:
            return []
        found = []
        for _, pieces in self.parts:
            if not any(pieces[-1][0] is value for value in found):
                found.append(pieces[-1][0])
        return found

    def exchange(self, value, stride):
        return lax.ppermute(value, "dp", [(i, i ^ stride) for i in range(self.count)])

    def advance(self, rounds, streams, other, tokens, name):
        arrays, specs, plan = [], [], []
        block, columns = self.block, self.columns
        blocks = 2 ** len(self.left(self.parts[0][0], rounds))
        for stream in streams:
            lengths = []
            for part in stream:
                order, pieces = self.parts[part]
                lengths.append(len(pieces))
                after = self.left(order, rounds)
                for value, place, since in pieces:
                    before = self.left(order, since)

                    def where(g, index, order=order, before=before, after=after, place=place):
                        bit = lambda value, at: lax.bitwise_and(lax.shift_right_logical(value, at), 1)
                        number = 0
                        for stride in before:
                            if stride in after:
                                chosen = bit(g, len(after) - 1 - after.index(stride))
                            else:
                                chosen = bit(index[0], stride.bit_length() - 1)
                                if other and stride == order[rounds - 1]:
                                    chosen = 1 - chosen
                            number = number * 2 + chosen
                        return place, number, 0, 0

                    arrays.append(value)
                    specs.append(pl.BlockSpec((1, 1, block, columns), where))
            plan.append(lengths)
        fresh = [i for i, value in enumerate(arrays) if any(value is p[-1][0] for _, p in self.parts)]
        gated = lax.optimization_barrier((self.index, tuple(arrays[i] for i in fresh), tuple(tokens)))
        for i, value in zip(fresh, gated[1]):
            arrays[i] = value
        arrays = [pltpu.with_memory_space_constraint(value, pltpu.HBM) for value in arrays]

        def body(_, *refs):
            refs = list(refs)
            for out, lengths in zip(refs[len(arrays):], plan):
                for place, amount in enumerate(lengths):
                    values = [refs.pop(0)[0, 0] for _ in range(amount)]
                    out[place, 0] = sum(values[1:], values[0])

        outs = [shape((len(stream), blocks, block, columns), F32) for stream in streams]
        return pl.pallas_call(
            body,
            name=name,
            grid_spec=pltpu.PrefetchScalarGridSpec(
                num_scalar_prefetch=1,
                grid=(blocks,),
                in_specs=specs,
                out_specs=[pl.BlockSpec((len(s), 1, block, columns), lambda g, _: (0, g, 0, 0)) for s in streams],
            ),
            out_shape=outs,
            compiler_params=pltpu.CompilerParams(vmem_limit_bytes=LIMIT),
        )(gated[0], *arrays)

    def step(self, *tokens):
        if not self.direct or self.round == len(self.parts[0][0]):
            return []
        self.round += 1
        strides = []
        for order, _ in self.parts:
            if order[self.round - 1] not in strides:
                strides.append(order[self.round - 1])
        streams = [[i for i, (order, _) in enumerate(self.parts) if order[self.round - 1] == stride]
                   for stride in strides]
        sends = self.advance(self.round, streams, True, tokens, "advance%d" % self.round)
        for stride, stream, send in zip(strides, streams, sends):
            arrived = self.exchange(send, stride)
            for place, part in enumerate(stream):
                self.parts[part][1].append((arrived, place, self.round))
        return list(sends)

    def finish(self, *tokens):
        if not self.direct:
            return [lax.psum_scatter(whole, "dp", scatter_dimension=0, tiled=True) for _, whole in self.parts]
        while self.round < len(self.parts[0][0]):
            self.step(*tokens)
        found = self.advance(self.round, [[i] for i in range(len(self.parts))], False, tokens, "settle")
        return [value.reshape(self.block, self.columns) for value in found]


def orders(count):
    bits = []
    bit = 1
    while bit < count:
        bits.append(bit)
        bit *= 2
    if len(bits) != 4:
        return bits, bits, bits
    return [1, 2, 4, 8], [2, 1, 4, 8], [4, 1, 2, 8]


def ring_orders(count):
    found = orders(count)
    return ([1, 2, 4, 8], [2, 4, 1, 8], [4, 1, 2, 8]) if count == 16 else found


def on_device(
    layer_in,
    memory,
    grad_out,
    seq_len,
    rel_bucket,
    self_gain,
    cross_gain,
    ffn_gain,
    rel_table,
    self_q,
    self_kv,
    self_o,
    cross_q,
    cross_kv,
    cross_o,
    ffn_in,
    ffn_out,
):
    buckets, heads = rel_table.shape
    width = self_q.shape[1]
    length = rel_bucket.shape[0]
    encoded = memory.shape[1]
    model = layer_in.shape[1]
    units = ffn_out.shape[0]
    seqs = seq_len.shape[0]
    half = model // lax.axis_size("mp")
    count = lax.axis_size("dp")
    side = lax.axis_index("mp").astype(jnp.int32).reshape(1)
    index = lax.axis_index("dp").astype(jnp.int32).reshape(1)
    table = jnp.zeros((8, LANES), F32).at[:heads, :buckets].set(rel_table.T)
    kv1 = self_kv.reshape(model, 2 * width)
    kv2 = cross_kv.reshape(model, 2 * width)
    w_in = ffn_in.reshape(model, 2 * units)
    gains = [g.reshape(1, model) for g in (self_gain, cross_gain, ffn_gain)]
    encoder = memory.reshape(seqs * encoded, model)
    across = range(seqs)
    rows = lambda array, s: (array, length, s)
    per = model // count
    ring = ring_orders(count)
    stage1 = []
    for s in across:
        stage1.append(call(
            functools.partial(self_forward, seq=s, width=width), "self_forward",
            [shape((length, model), F32), shape((length, model), BF16), shape((length, 3 * width), BF16),
             shape((length, width), BF16), shape((length, LANES), F32)],
            [seq_len, rows(layer_in, s), gains[0], self_q, kv1, self_o, table, rel_bucket],
            smem=1, keep=(1, 2, 3, 4),
        ))
    swapped1 = [swap(found[0]) for found in stage1]
    encoded_kv = [
        call(project, "encoder_kv", [shape((encoded, 2 * width), BF16)], [rows(encoder, s), kv2])[0]
        for s in across
    ]
    stage2 = []
    for s in across:
        stage2.append(call(
            functools.partial(cross_forward, width=width), "cross_forward",
            [shape((length, model), F32), shape((length, model), F32), shape((length, model), BF16),
             shape((length, width), BF16), shape((length, width), BF16), shape((length, LANES), F32)],
            [rows(layer_in, s), stage1[s][0], swapped1[s], gains[1], cross_q, cross_o, encoded_kv[s]],
            keep=(2, 3, 4, 5),
        ))
    swapped2 = [swap(found[0]) for found in stage2]
    stage3, joint = [], None
    for s in across:
        stage3.append(call(
            ffn_both, "ffn_both",
            [shape((length, half), F32), shape((length, model), F32),
             shape((length, model), BF16), shape((length, units), BF16), shape((length, 2 * units), BF16),
             shape((length, model + half), F32)],
            [side, stage2[s][1], stage2[s][0], swapped2[s], gains[2], rows(grad_out, s), w_in, ffn_out],
            scratch=[pltpu.VMEM((length, model), F32)],
            smem=1, keep=(0, 2, 3, 4), shared=(5, s, joint, seqs),
        ))
        joint = stage3[s][5]
    swapped3 = swap(joint)
    grad3 = joint
    normed3 = [found[2] for found in stage3]
    dgus = [found[4] for found in stage3]
    ffn = Group(index, per, units)
    after = ffn.add(
        [(grad_out, s) for s in across], [found[3] for found in stage3], ring[1], "grad_ffn_out", [joint])
    after = ffn.add(normed3, dgus, ring[0], "grad_gate", after, 0, units)
    after = ffn.add(normed3, dgus, ring[2], "grad_up", after, units, units)
    back_scratch = [
        pltpu.VMEM((length, width), BF16), pltpu.VMEM((width, length), BF16), pltpu.VMEM((width, length), BF16),
        pltpu.VMEM((width, length), F32), pltpu.VMEM((width, length), F32),
    ]
    stage4, joint = [], None
    for s in across:
        stage4.append(call(
            functools.partial(cross_backward, width=width), "cross_backward",
            [shape((length, model), F32), shape((length, model), F32), shape((length, model), BF16),
             shape((length, 3 * width), BF16), shape((encoded, half), F32), shape((1, model), F32),
             shape((encoded, half), F32)],
            [gate(side, *after), rows(grad_out, s), (grad3, length, s, model), (swapped3, length, s, model),
             stage3[s][1], gains[2], stage2[s][3], encoded_kv[s], stage2[s][5], cross_q, kv2, cross_o],
            scratch=back_scratch + [pltpu.VMEM((encoded, model), F32)],
            smem=1, keep=(4, 6), shared=(6, s, joint, seqs),
        ))
        joint = stage4[s][6]
        after = [stage4[s][5]]
    rest4 = joint
    swapped4 = [swap(found[0]) for found in stage4]
    pair = lambda found: [(value, 0) for value in found]
    both = Group(index, per, width + width // 3)
    after, launch = both.add_attention(
        pair([found[2] for found in stage2]), [(encoder, s) for s in across], pair([found[2] for found in stage4]),
        [found[3] for found in stage4], [found[4] for found in stage2], "grad_cross", after)
    after = ffn.step(*after)
    stage5, joint = [], None
    for s in across:
        stage5.append(call(
            functools.partial(self_backward, seq=s, width=width), "self_backward",
            [shape((length, model), F32), shape((length, model), F32), shape((length, model), BF16),
             shape((length, 3 * width), BF16), shape((heads, length, length), BF16), shape((1, model), F32)],
            [gate(seq_len, *after), stage4[s][1], stage4[s][0], swapped4[s],
             stage2[s][1], gains[1], stage1[s][2], stage1[s][4], self_q, kv1, self_o, table, rel_bucket],
            scratch=back_scratch,
            smem=1, shared=(0, s, joint, seqs), direct=s == 0,
        ))
        joint = stage5[s][0]
        after = [stage5[s][5]]
        if s == 0:
            launch(*after, *ffn.arrivals())
    grad5 = joint
    swapped5 = swap(gate(grad5, *both.arrivals()))
    after = ffn.step(*after, *both.arrivals())
    normed1 = pair([found[1] for found in stage1])
    after, launch = both.add_attention(
        normed1, normed1, pair([found[2] for found in stage5]),
        [found[3] for found in stage5], [found[3] for found in stage1], "grad_self", after)
    launch(swapped5, *ffn.arrivals())
    after = ffn.step(swapped5, *after)
    stage6, joint = [], None
    for s in across:
        stage6.append(call(
            input_backward, "input_backward",
            [shape((length, model), F32), shape((1, model), F32)],
            [stage5[s][1], rows(grad5, s), rows(swapped5, s), rows(layer_in, s), gate(gains[0], *after)],
            keep=(0,), shared=(0, s, joint, seqs),
        ))
        joint = stage6[s][0]
        after = [stage6[s][1]]
    grad_layer_in = joint
    swapped6 = swap(gate(rest4, *after))
    spread = call(
        functools.partial(table_backward, buckets=buckets), "table_backward",
        [shape((2 * heads * 8, 8 * buckets), F32)],
        [gate(index, *after), rel_bucket, stage5[0][4], stage5[1][4]],
        scratch=[pltpu.VMEM((2 * heads * 8, 8 * buckets), F32)], smem=1,
    )[0]
    table_grad = spread.reshape(2, heads, 8, 8, buckets).sum(axis=(0, 2, 3)).T
    after = both.step(spread, *ffn.arrivals())
    grad_w_out, grad_gate, grad_up = ffn.finish(spread, *after)
    gain1 = sum(found[1] for found in stage6)
    gain2 = sum(found[5] for found in stage5)
    gain3 = sum(found[5] for found in stage4)
    small = jnp.concatenate([gain1[0], gain2[0], gain3[0], table_grad.reshape(-1)])
    bits = sorted(orders(count)[0], reverse=True)
    arrived = dp_swap(small, bits[0])
    for bit in bits[1:-2]:
        after = both.step(*both.arrivals(), arrived)
        small = small + gate(arrived, *after)
        arrived = dp_swap(small, bit)
    after = both.step(*both.arrivals(), arrived)
    small = small + gate(arrived, *after)
    for bit in bits[-2:]:
        small = small + dp_swap(small, bit)
    theirs3 = gate(swapped3, spread, *after)
    theirs4 = gate(swapped6, *after)
    mixed = jnp.concatenate([found[0] for found in stage3], axis=0)
    mixed = (mixed + theirs3[:, model:]).astype(BF16)
    grad_memory = jnp.concatenate([found[4] for found in stage4], axis=0) + theirs4
    grad_memory = grad_memory.reshape(seqs, encoded, half)
    settled = both.finish()
    results = []
    for first in (0, 3):
        q, k, v = [value[:, :width] for value in settled[first : first + 3]]
        o = jnp.concatenate([value[:, width:] for value in settled[first : first + 3]], axis=1)
        results.append((q, jnp.stack([k, v], axis=1), o))
    (grad_cross_q, grad_cross_kv, grad_cross_o), (grad_self_q, grad_self_kv, grad_self_o) = results
    begin = index[0] * per
    gain_grads = [lax.dynamic_slice_in_dim(small, i * model + begin, per, 0) for i in range(3)]
    grad_table = small[3 * model :].reshape(buckets, heads)
    return (
        mixed,
        grad_layer_in,
        grad_memory,
        *gain_grads,
        grad_table,
        grad_self_q,
        grad_self_kv,
        grad_self_o.T,
        grad_cross_q,
        grad_cross_kv,
        grad_cross_o.T,
        jnp.stack([grad_gate, grad_up], axis=1),
        grad_w_out.T,
    )


def solution(mesh):
    placed = (
        P("dp", None),
        P("dp", None, None),
        P("dp", None),
        P("dp"),
        P(),
        P(),
        P(),
        P(),
        P(None, "mp"),
        P(None, "mp"),
        P(None, None, "mp"),
        P("mp", None),
        P(None, "mp"),
        P(None, None, "mp"),
        P("mp", None),
        P(None, None, "mp"),
        P("mp", None),
    )
    return jax.shard_map(
        on_device,
        mesh=mesh,
        in_specs=placed,
        out_specs=(
            P("dp", "mp"),
            P("dp", None),
            P("dp", None, "mp"),
            P("dp"),
            P("dp"),
            P("dp"),
            P(None, "mp"),
            P("dp", "mp"),
            P("dp", None, "mp"),
            P("mp", "dp"),
            P("dp", "mp"),
            P("dp", None, "mp"),
            P("mp", "dp"),
            P("dp", None, "mp"),
            P("mp", "dp"),
        ),
        check_vma=False,
    )
```

```python
import functools

import jax
import jax.numpy as jnp
from jax import lax
from jax.experimental import pallas as pl
from jax.experimental.pallas import tpu as pltpu
from jax.sharding import PartitionSpec as P

EPS = 1e-06
NEGATIVE = -1e30
F32 = jnp.float32
BF16 = jnp.bfloat16
LANES = 128
QB = 256
TB = 128
QC = 512
LIMIT = 26 * 2**20


def nn(left, right):
    return lax.dot_general(left, right, (((1,), (0,)), ((), ())), preferred_element_type=F32)


def nt(left, right):
    return lax.dot_general(left, right, (((1,), (1,)), ((), ())), preferred_element_type=F32)


def norm(values, gain):
    inverse = lax.rsqrt(jnp.mean(values * values, axis=-1, keepdims=True) + EPS)
    scaled = values * inverse
    return scaled * gain, scaled, inverse


def norm_back(grad, values, gain):
    inverse = lax.rsqrt(jnp.mean(values * values, axis=-1, keepdims=True) + EPS)
    scaled = values * inverse
    grad_scaled = grad * gain
    inner = jnp.mean(grad_scaled * scaled, axis=-1, keepdims=True)
    gain_grad = jnp.sum(grad * scaled, axis=0, keepdims=True)
    return inverse * (grad_scaled - scaled * inner), gain_grad


def own_half(value, side):
    lane = lax.broadcasted_iota(jnp.int32, value.shape, 1)
    keep = lane < LANES // 2 if side == 0 else lane >= LANES // 2
    return jnp.where(keep, value, jnp.zeros_like(value))


def join_halves(first, second):
    lane = lax.broadcasted_iota(jnp.int32, first.shape, 1)
    return jnp.where(lane < LANES // 2, first, second)


def bias_of(table_ref, bucket_ref, head, start, rows, keys):
    row = jnp.broadcast_to(table_ref[pl.ds(head, 1), :], (rows, LANES))
    parts = []
    for first in range(0, keys, LANES):
        index = bucket_ref[start : start + rows, first : first + LANES]
        parts.append(jnp.take_along_axis(row, index, axis=1, mode="promise_in_bounds"))
    return jnp.concatenate(parts, axis=1) if len(parts) > 1 else parts[0]


def masked(raw, start, count):
    rows, keys = raw.shape
    place = lax.broadcasted_iota(jnp.int32, (rows, 1), 0) + (start + 1)
    limit = jnp.minimum(place, count)
    column = lax.broadcasted_iota(jnp.int32, raw.shape, 1)
    return jnp.where(column < limit, raw, NEGATIVE)


def attend(q_ref, k_ref, v_ref, c_ref, lse_ref, length, keys_all, score, block=QB):
    pairs = q_ref.shape[1] // LANES
    lane = lax.broadcasted_iota(jnp.int32, (block, LANES), 1)

    def one_pair(pair, carry):
        columns = pl.ds(pl.multiple_of(pair * LANES, LANES), LANES)
        for start in range(0, length, block):
            keys = keys_all(start)
            query = q_ref[start : start + block, columns]
            key = k_ref[0:keys, columns]
            value = v_ref[0:keys, columns]
            found = []
            kept = lse_ref[start : start + block, :]
            for side in range(2):
                head = pair * 2 + side
                raw = score(nt(own_half(query, side), key), head, start)
                top = jnp.max(raw, axis=1, keepdims=True)
                weight = jnp.exp(raw - top)
                total = jnp.sum(weight, axis=1, keepdims=True)
                probs = (weight * (1.0 / total)).astype(BF16)
                found.append(nn(probs, value))
                kept = jnp.where(lane == head, top + jnp.log(total), kept)
            lse_ref[start : start + block, :] = kept
            c_ref[start : start + block, columns] = join_halves(*found).astype(BF16)
        return carry

    lse_ref[...] = jnp.zeros_like(lse_ref)
    lax.fori_loop(0, pairs, one_pair, 0)


def attend_back(q_ref, k_ref, v_ref, dc_ref, lse_ref, d_ref, qt, dct, dkt, dvt, ds_ref, length, keys_all, score, block=QB):
    width = q_ref.shape[1]
    pairs = width // LANES
    lane = lax.broadcasted_iota(jnp.int32, (block, LANES), 1)
    qt[...] = q_ref[...].T
    dct[...] = dc_ref[...].T
    half = LANES // 2

    def one_pair(pair, carry):
        columns = pl.ds(pl.multiple_of(pair * LANES, LANES), LANES)
        for start in range(0, length, block):
            rows = slice(start, start + block)
            keys = keys_all(start)
            query = q_ref[rows, columns]
            grad = dc_ref[rows, columns]
            key = k_ref[0:keys, columns]
            value = v_ref[0:keys, columns]
            lse_all = lse_ref[rows, :]
            found = []
            for side in range(2):
                head = pair * 2 + side
                lse = jnp.sum(jnp.where(lane == head, lse_all, 0.0), axis=1, keepdims=True)
                raw = score(nt(own_half(query, side), key), head, start)
                probs = jnp.exp(raw - lse)
                grad_probs = nt(own_half(grad, side), value)
                inner = jnp.sum(probs * grad_probs, axis=1, keepdims=True)
                low = probs.astype(BF16)
                grad_raw = (probs * (grad_probs - inner)).astype(BF16)
                if ds_ref is not None:
                    ds_ref[pl.ds(head, 1), rows, 0:keys] = grad_raw[None]
                found.append(nn(grad_raw, key))
                place = pl.ds(pl.multiple_of(pair * LANES + side * half, half), half)
                add_k = nn(qt[place, rows], grad_raw)
                add_v = nn(dct[place, rows], low)
                if start == 0:
                    dkt[place, 0:keys] = add_k
                    dvt[place, 0:keys] = add_v
                else:
                    before = keys_all(start - block)
                    dkt[place, 0:before] += add_k[:, 0:before]
                    dvt[place, 0:before] += add_v[:, 0:before]
                    if before < keys:
                        dkt[place, before:keys] = add_k[:, before:keys]
                        dvt[place, before:keys] = add_v[:, before:keys]
            d_ref[rows, columns] = join_halves(*found).astype(BF16)
        return carry

    lax.fori_loop(0, pairs, one_pair, 0)
    d_ref[:, width : 2 * width] = dkt[...].astype(BF16).T
    d_ref[:, 2 * width : 3 * width] = dvt[...].astype(BF16).T


def causal_keys(start):
    return start + QB


def self_forward(len_ref, x_ref, gain_ref, wq_ref, wkv_ref, wo_ref, table_ref, bucket_ref,
                 part_ref, n_ref, qkv_ref, c_ref, lse_ref, *, seq, width):
    length = x_ref.shape[0]
    normed, _, _ = norm(x_ref[...].astype(F32), gain_ref[...])
    n_ref[...] = normed.astype(BF16)
    qkv_ref[:, 0:width] = nn(n_ref[...], wq_ref[...]).astype(BF16)
    qkv_ref[:, width:] = nn(n_ref[...], wkv_ref[...]).astype(BF16)
    count = len_ref[seq]

    def score(raw, head, start):
        biased = raw + bias_of(table_ref, bucket_ref, head, start, *raw.shape)
        return masked(biased, start, count)

    attend(qkv_ref.at[:, 0:width], qkv_ref.at[:, width : 2 * width], qkv_ref.at[:, 2 * width : 3 * width],
           c_ref, lse_ref, length, causal_keys, score)
    part_ref[...] = nn(c_ref[...], wo_ref[...])


def project(x_ref, w_ref, out_ref):
    out_ref[...] = nn(x_ref[...], w_ref[...]).astype(out_ref.dtype)


def cross_forward(x_ref, mine_ref, theirs_ref, gain_ref, wq_ref, wo_ref, kv_ref,
                  part_ref, h_ref, n_ref, q_ref, c_ref, lse_ref, *, width):
    hidden = x_ref[...].astype(F32) + (mine_ref[...] + theirs_ref[...])
    h_ref[...] = hidden
    normed, _, _ = norm(hidden, gain_ref[...])
    n_ref[...] = normed.astype(BF16)
    q_ref[...] = nn(n_ref[...], wq_ref[...]).astype(BF16)
    keys = kv_ref.shape[0]
    attend(q_ref, kv_ref.at[:, 0:width], kv_ref.at[:, width : 2 * width], c_ref, lse_ref,
           x_ref.shape[0], lambda start: keys, lambda raw, head, start: raw, QC)
    part_ref[...] = nn(c_ref[...], wo_ref[...])


GELU_C = 0.7978845608028654
GELU_A = 0.044715


def ffn_both(side_ref, h_ref, mine_ref, theirs_ref, gain_ref, dy_ref, win_ref, wout_ref,
             mixed_ref, h2_ref, n_ref, inner_ref, dgu_ref, dn_ref, scratch):
    hidden = h_ref[...] + (mine_ref[...] + theirs_ref[...])
    h2_ref[...] = hidden
    normed, _, _ = norm(hidden, gain_ref[...])
    n_ref[...] = normed.astype(BF16)
    units = wout_ref.shape[0]
    step = 256

    def one(chunk, carry):
        first = pl.multiple_of(chunk * step, step)
        here = pl.ds(first, step)
        there = pl.ds(pl.multiple_of(units + chunk * step, step), step)
        gate = nn(n_ref[...], win_ref[:, here])
        upward = nn(n_ref[...], win_ref[:, there])
        grad = nt(dy_ref[...], wout_ref[here, :])
        squared = gate * gate
        bent = jnp.tanh(gate * (GELU_C + (GELU_C * GELU_A) * squared))
        half = 0.5 + 0.5 * bent
        soft = gate * half
        slope = half + (0.5 * gate) * (1.0 - bent * bent) * (GELU_C + (3 * GELU_C * GELU_A) * squared)
        inner_ref[:, here] = (soft * upward).astype(BF16)
        dgu_ref[:, here] = (grad * upward * slope).astype(BF16)
        dgu_ref[:, there] = (grad * soft).astype(BF16)
        return carry

    lax.fori_loop(0, units // step, one, 0)
    model = h_ref.shape[1]
    dn_ref[:, 0:model] = nt(dgu_ref[...], win_ref[...])
    share = nn(inner_ref[...], wout_ref[...])
    scratch[...] = share
    half = mixed_ref.shape[1]
    me = side_ref[0]
    mine = pl.ds(pl.multiple_of(me * half, LANES), half)
    other = pl.ds(pl.multiple_of((1 - me) * half, LANES), half)
    mixed_ref[...] = h2_ref[:, mine] + scratch[:, mine]
    dn_ref[:, model:] = scratch[:, other]


def cross_backward(side_ref, dy_ref, mine_ref, theirs_ref, h_ref, gain_ref, q_ref, kv_ref, lse_ref,
                   wq_ref, wkv_ref, wo_ref,
                   dn_ref, dh_ref, da_ref, d_ref, gm_ref, gain_out_ref, go_ref,
                   dc, qt, dct, dkt, dvt, scratch, *, width):
    back, gain_grad = norm_back(mine_ref[...] + theirs_ref[...], h_ref[...], gain_ref[...])
    gain_out_ref[...] = gain_grad
    grad = dy_ref[...].astype(F32) + back
    dh_ref[...] = grad
    da_ref[...] = grad.astype(BF16)
    dc[...] = nt(da_ref[...], wo_ref[...]).astype(BF16)
    keys = kv_ref.shape[0]
    attend_back(q_ref, kv_ref.at[:, 0:width], kv_ref.at[:, width : 2 * width], dc, lse_ref, d_ref,
                qt, dct, dkt, dvt, None, dy_ref.shape[0], lambda start: keys, lambda raw, head, start: raw, QC)
    dn_ref[...] = nt(d_ref[:, 0:width], wq_ref[...])
    scratch[...] = nt(d_ref[:, width : 3 * width], wkv_ref[...])
    half = gm_ref.shape[1]
    me = side_ref[0]
    gm_ref[...] = scratch[:, pl.ds(pl.multiple_of(me * half, LANES), half)]
    go_ref[...] = scratch[:, pl.ds(pl.multiple_of((1 - me) * half, LANES), half)]


def self_backward(len_ref, before_ref, mine_ref, theirs_ref, h_ref, gain_ref, qkv_ref, lse_ref,
                  wq_ref, wkv_ref, wo_ref, table_ref, bucket_ref,
                  dn_ref, dh_ref, da_ref, d_ref, ds_ref, gain_out_ref,
                  dc, qt, dct, dkt, dvt, *, seq, width):
    back, gain_grad = norm_back(mine_ref[...] + theirs_ref[...], h_ref[...], gain_ref[...])
    gain_out_ref[...] = gain_grad
    grad = before_ref[...] + back
    dh_ref[...] = grad
    da_ref[...] = grad.astype(BF16)
    dc[...] = nt(da_ref[...], wo_ref[...]).astype(BF16)
    count = len_ref[seq]

    def score(raw, head, start):
        biased = raw + bias_of(table_ref, bucket_ref, head, start, *raw.shape)
        return masked(biased, start, count)

    attend_back(qkv_ref.at[:, 0:width], qkv_ref.at[:, width : 2 * width], qkv_ref.at[:, 2 * width : 3 * width],
                dc, lse_ref, d_ref, qt, dct, dkt, dvt, ds_ref, h_ref.shape[0],
                lambda start: start + QC, score, QC)
    dn_ref[...] = nt(d_ref[:, 0:width], wq_ref[...]) + nt(d_ref[:, width : 3 * width], wkv_ref[...])


def input_backward(before_ref, mine_ref, theirs_ref, x_ref, gain_ref, out_ref, gain_out_ref):
    back, gain_grad = norm_back(mine_ref[...] + theirs_ref[...], x_ref[...].astype(F32), gain_ref[...])
    gain_out_ref[...] = gain_grad
    out_ref[...] = before_ref[...] + back


def table_backward(_, bucket_ref, first_ref, second_ref, out_ref, total, *, buckets):
    heads, length, _ = first_ref.shape
    group = 8

    def one(block, carry, keys):
        start = pl.multiple_of(block * group, group)
        rows = pl.ds(start, group)
        code = bucket_ref[rows, 0:keys]
        spread = lax.broadcasted_iota(jnp.int32, (buckets, keys), 0)
        column = lax.broadcasted_iota(jnp.int32, (1, keys), 1)
        pieces = []
        for i in range(group):
            seen = jnp.where(column <= start + i, code[i : i + 1, :], -1)
            pieces.append((spread == seen).astype(F32))
        chosen = jnp.concatenate(pieces, axis=0).astype(BF16)
        both = []
        for ref in (first_ref, second_ref):
            values = ref[:, rows, 0:keys].astype(F32)
            both.append(values.reshape(heads * group, keys))
        total[...] += nt(jnp.concatenate(both, axis=0).astype(BF16), chosen)
        return carry

    total[...] = jnp.zeros_like(total)
    for start in range(0, length, TB):
        lax.fori_loop(start // group, (start + TB) // group, functools.partial(one, keys=start + TB), 0)
    row = lax.broadcasted_iota(jnp.int32, total.shape, 0)
    column = lax.broadcasted_iota(jnp.int32, total.shape, 1)
    out_ref[...] = jnp.where(lax.rem(row, group) == column // buckets, total[...], 0.0)


def weight_grad(index_ref, l0_ref, l1_ref, r0_ref, r1_ref, *rest, stride, blocks):
    outs, (turned, scratch) = rest[:-2], rest[-2:]
    length = l0_ref.shape[0]

    @pl.when(pl.program_id(0) == 0)
    def _():
        turned[:, 0:length] = l0_ref[...].T
        turned[:, length : 2 * length] = l1_ref[...].T

    value = nn(turned[:, 0:length], r0_ref[...]) + nn(turned[:, length : 2 * length], r1_ref[...])
    if stride is None:
        outs[0][...] = value
        return
    scratch[...] = value
    keep_ref, send_ref = outs
    block = scratch.shape[0] // blocks
    bit = lax.rem(index_ref[0] // stride, 2)
    for place in range(blocks // 2):
        low, high = place % stride, place // stride
        base = high * 2 * stride + low
        mine = pl.multiple_of((base + bit * stride) * block, 8)
        other = pl.multiple_of((base + (1 - bit) * stride) * block, 8)
        keep_ref[0, place] = scratch[pl.ds(mine, block), :]
        send_ref[0, place] = scratch[pl.ds(other, block), :]


def attention_grads(index_ref, *refs, strides, blocks, same):
    a0, a1, b0, b1, c0, c1, d0, d1, e0, e1 = refs[:10]
    outs, (turned, other, scratch) = refs[10:-3], refs[-3:]
    length, width = d0.shape
    step = pl.program_id(0)

    def turn(target, first, second):
        target[:, 0:length] = first[...].T
        target[:, length : 2 * length] = second[...].T

    @pl.when(step == 0)
    def _():
        turn(turned, a0, a1)
        turn(other, c0, c1)

    if not same:
        @pl.when(step == 1)
        def _():
            turn(turned, b0, b1)

    near, far = slice(0, length), slice(length, 2 * length)
    target = scratch if strides is not None else outs[0]
    target[:, 0:width] = nn(turned[:, near], d0[...]) + nn(turned[:, far], d1[...])
    target[:, width:] = nn(other[:, near], e0[...]) + nn(other[:, far], e1[...])
    if strides is None:
        return
    keep_ref, sends = outs[0], outs[1:]
    block = scratch.shape[0] // blocks
    for part, stride in enumerate(strides):
        @pl.when(step == part)
        def _(part=part, stride=stride):
            bit = lax.rem(index_ref[0] // stride, 2)
            for place in range(blocks // 2):
                low, high = place % stride, place // stride
                base = high * 2 * stride + low
                mine = pl.multiple_of((base + bit * stride) * block, 8)
                theirs = pl.multiple_of((base + (1 - bit) * stride) * block, 8)
                keep_ref[0, place] = scratch[pl.ds(mine, block), :]
                sends[part][0, place] = scratch[pl.ds(theirs, block), :]


def call(body, name, outs, args, scratch=(), smem=0, keep=(), shared=None, direct=False):
    in_specs, arrays = [], []
    for place, value in enumerate(args):
        if place < smem:
            in_specs.append(pl.BlockSpec(memory_space=pltpu.SMEM))
            arrays.append(value)
            continue
        array, size, block, columns = value, value.shape[0] if not isinstance(value, tuple) else 0, 0, None
        if isinstance(value, tuple):
            array, size, block = value[:3]
            columns = value[3] if len(value) > 3 else None
        dims = (size,) + array.shape[1:] if columns is None else (size, columns)
        where = (block,) + (0,) * (array.ndim - 1)
        in_specs.append(pl.BlockSpec(dims, lambda i, where=where: where, pipeline_mode=pl.Buffered(1)))
        arrays.append(array)
    shapes, out_specs, aliases = [], [], {}
    for place, out in enumerate(outs):
        dims, where = out.shape, (0,) * len(out.shape)
        if shared is not None and place == shared[0]:
            where = (shared[1],) + where[1:]
            out = shape((shared[3] * dims[0],) + dims[1:], out.dtype)
        out_specs.append(pl.BlockSpec(dims, lambda i, where=where: where, pipeline_mode=pl.Buffered(1)))
        shapes.append(pltpu.HBM(out.shape, out.dtype) if place in keep else out)
    used = len(arrays)
    if shared is not None and shared[2] is not None:
        aliases[used] = shared[0]
        in_specs.append(pl.BlockSpec(memory_space=pl.ANY))
        arrays.append(shared[2])
    extra = len(arrays) - used
    if direct:
        arrays[smem:used] = [pltpu.with_memory_space_constraint(a, pltpu.HBM) for a in arrays[smem:used]]

    def run(*refs):
        body(*refs[:used], *refs[used + extra :])

    return pl.pallas_call(
        run,
        name=name,
        grid=(1,),
        out_shape=shapes,
        in_specs=in_specs,
        out_specs=out_specs,
        scratch_shapes=list(scratch),
        input_output_aliases=aliases,
        compiler_params=pltpu.CompilerParams(vmem_limit_bytes=LIMIT),
    )(*arrays)


def shape(dims, dtype):
    return jax.ShapeDtypeStruct(dims, dtype)


def gate(value, *tokens):
    return lax.optimization_barrier((value,) + tokens)[0]


def swap(value):
    size = lax.axis_size("mp")
    return lax.ppermute(value, "mp", [(i, size - 1 - i) for i in range(size)])


def dp_swap(value, bit):
    return lax.ppermute(value, "dp", [(i, i ^ bit) for i in range(lax.axis_size("dp"))])


class Group:
    def __init__(self, index, block, columns):
        self.index, self.block, self.columns = index, block, columns
        self.count = lax.axis_size("dp")
        self.direct = block % 8 == 0 and self.count > 1
        self.round = 1
        self.parts = []
        self.tokens = []

    def left(self, order, rounds):
        return sorted(set(order) - set(order[:rounds]), reverse=True)

    def add(self, lefts, rights, order, name, after, first=0, columns=None):
        parts = [value if isinstance(value, tuple) else (value, 0) for value in lefts]
        lefts = [value for value, _ in parts]
        length, model = rights[0].shape[0], lefts[0].shape[1]
        columns = rights[0].shape[1] if columns is None else columns
        step = self.columns
        width = step if step % 512 else 512
        if self.direct:
            half = (columns // step, self.count // 2, self.block, step)
            outs = [pltpu.HBM(half, F32)] * 2
            per = step // width
            out_specs = [pl.BlockSpec((1,) + half[1:3] + (width,), lambda j: (j // per, 0, 0, j % per))] * 2
        else:
            outs = [shape((model, columns), F32)]
            out_specs = [pl.BlockSpec((model, width), lambda j: (0, j))]
        skip = first // width
        found = pl.pallas_call(
            functools.partial(weight_grad, stride=order[0] if self.direct else None, blocks=self.count),
            name=name,
            grid=(columns // width,),
            out_shape=outs,
            in_specs=[pl.BlockSpec(memory_space=pltpu.SMEM)]
            + [pl.BlockSpec((length, model), lambda j, place=place: (place, 0)) for _, place in parts]
            + [pl.BlockSpec((length, width), lambda j: (0, j + skip))] * 2,
            out_specs=out_specs,
            scratch_shapes=[pltpu.VMEM((model, 2 * length), BF16), pltpu.VMEM((model, width), F32)],
            compiler_params=pltpu.CompilerParams(vmem_limit_bytes=LIMIT),
        )(gate(self.index, *after), *lefts, *rights)
        if not self.direct:
            for start in range(0, columns, step):
                self.parts.append((order, found[0][:, start : start + step]))
            return [found[0]]
        keep, send = found
        arrived = self.exchange(send, order[0])
        for place in range(columns // step):
            self.parts.append((order, [(keep, place, 1), (arrived, place, 1)]))
        return [send]

    def add_attention(self, normed, keyed, grads, d, c, name, after):
        arrays = [value for pair in (normed, keyed, grads) for value, _ in pair]
        places = [place for pair in (normed, keyed, grads) for _, place in pair]
        length, width = c[0].shape
        model, third = arrays[0].shape[1], width // 3
        columns = self.columns
        orders = ring_orders(self.count)
        half = (1, self.count // 2, self.block, columns)
        fixed = lambda j: (0, 0, 0, 0)
        if self.direct:
            outs = [pltpu.HBM((3,) + half[1:], F32)] + [pltpu.HBM(half, F32)] * 3
            out_specs = [pl.BlockSpec(half, lambda j: (j, 0, 0, 0))] + [pl.BlockSpec(half, fixed)] * 3
        else:
            outs = [shape((model, 3 * columns), F32)]
            out_specs = [pl.BlockSpec((model, columns), lambda j: (0, j))]
        found = pl.pallas_call(
            functools.partial(
                attention_grads, strides=[order[0] for order in orders] if self.direct else None,
                blocks=self.count, same=normed is keyed),
            name=name,
            grid=(3,),
            out_shape=outs,
            in_specs=[pl.BlockSpec(memory_space=pltpu.SMEM)]
            + [pl.BlockSpec((length, model), lambda j, place=place: (place, 0)) for place in places]
            + [pl.BlockSpec((length, width), lambda j: (0, j))] * 2
            + [pl.BlockSpec((length, third), lambda j: (0, j))] * 2,
            out_specs=out_specs,
            scratch_shapes=[pltpu.VMEM((model, 2 * length), BF16)] * 2 + [pltpu.VMEM((model, columns), F32)],
            compiler_params=pltpu.CompilerParams(vmem_limit_bytes=40 * 2**20),
        )(gate(self.index, *after), *arrays, *d, *c)
        if not self.direct:
            for part, order in enumerate(orders):
                self.parts.append((order, found[0][:, part * columns : (part + 1) * columns]))
            return [found[0]], lambda *tokens: None

        def launch(*tokens):
            sends = lax.optimization_barrier((tuple(found[1:]), tokens))[0]
            for part, order in enumerate(orders):
                arrived = self.exchange(sends[part], order[0])
                self.parts.append((order, [(found[0], part, 1), (arrived, 0, 1)]))

        return list(found[1:]), launch

    def arrivals(self):
        if not self.direct:
            return []
        found = []
        for _, pieces in self.parts:
            if not any(pieces[-1][0] is value for value in found):
                found.append(pieces[-1][0])
        return found

    def exchange(self, value, stride):
        return lax.ppermute(value, "dp", [(i, i ^ stride) for i in range(self.count)])

    def advance(self, rounds, streams, other, tokens, name):
        arrays, specs, plan = [], [], []
        block, columns = self.block, self.columns
        blocks = 2 ** len(self.left(self.parts[0][0], rounds))
        for stream in streams:
            lengths = []
            for part in stream:
                order, pieces = self.parts[part]
                lengths.append(len(pieces))
                after = self.left(order, rounds)
                for value, place, since in pieces:
                    before = self.left(order, since)

                    def where(g, index, order=order, before=before, after=after, place=place):
                        bit = lambda value, at: lax.bitwise_and(lax.shift_right_logical(value, at), 1)
                        number = 0
                        for stride in before:
                            if stride in after:
                                chosen = bit(g, len(after) - 1 - after.index(stride))
                            else:
                                chosen = bit(index[0], stride.bit_length() - 1)
                                if other and stride == order[rounds - 1]:
                                    chosen = 1 - chosen
                            number = number * 2 + chosen
                        return place, number, 0, 0

                    arrays.append(value)
                    specs.append(pl.BlockSpec((1, 1, block, columns), where))
            plan.append(lengths)
        fresh = [i for i, value in enumerate(arrays) if any(value is p[-1][0] for _, p in self.parts)]
        gated = lax.optimization_barrier((self.index, tuple(arrays[i] for i in fresh), tuple(tokens)))
        for i, value in zip(fresh, gated[1]):
            arrays[i] = value
        arrays = [pltpu.with_memory_space_constraint(value, pltpu.HBM) for value in arrays]

        def body(_, *refs):
            refs = list(refs)
            for out, lengths in zip(refs[len(arrays):], plan):
                for place, amount in enumerate(lengths):
                    values = [refs.pop(0)[0, 0] for _ in range(amount)]
                    out[place, 0] = sum(values[1:], values[0])

        outs = [shape((len(stream), blocks, block, columns), F32) for stream in streams]
        return pl.pallas_call(
            body,
            name=name,
            grid_spec=pltpu.PrefetchScalarGridSpec(
                num_scalar_prefetch=1,
                grid=(blocks,),
                in_specs=specs,
                out_specs=[pl.BlockSpec((len(s), 1, block, columns), lambda g, _: (0, g, 0, 0)) for s in streams],
            ),
            out_shape=outs,
            compiler_params=pltpu.CompilerParams(vmem_limit_bytes=LIMIT),
        )(gated[0], *arrays)

    def step(self, *tokens):
        if not self.direct or self.round == len(self.parts[0][0]):
            return []
        self.round += 1
        strides = []
        for order, _ in self.parts:
            if order[self.round - 1] not in strides:
                strides.append(order[self.round - 1])
        streams = [[i for i, (order, _) in enumerate(self.parts) if order[self.round - 1] == stride]
                   for stride in strides]
        sends = self.advance(self.round, streams, True, tokens, "advance%d" % self.round)
        for stride, stream, send in zip(strides, streams, sends):
            arrived = self.exchange(send, stride)
            for place, part in enumerate(stream):
                self.parts[part][1].append((arrived, place, self.round))
        return list(sends)

    def finish(self, *tokens):
        if not self.direct:
            return [lax.psum_scatter(whole, "dp", scatter_dimension=0, tiled=True) for _, whole in self.parts]
        while self.round < len(self.parts[0][0]):
            self.step(*tokens)
        found = self.advance(self.round, [[i] for i in range(len(self.parts))], False, tokens, "settle")
        return [value.reshape(self.block, self.columns) for value in found]


def orders(count):
    bits = []
    bit = 1
    while bit < count:
        bits.append(bit)
        bit *= 2
    if len(bits) != 4:
        return bits, bits, bits
    return [1, 2, 4, 8], [2, 1, 4, 8], [4, 1, 2, 8]


def ring_orders(count):
    found = orders(count)
    return ([1, 2, 4, 8], [2, 4, 1, 8], [4, 1, 2, 8]) if count == 16 else found


def on_device(
    layer_in,
    memory,
    grad_out,
    seq_len,
    rel_bucket,
    self_gain,
    cross_gain,
    ffn_gain,
    rel_table,
    self_q,
    self_kv,
    self_o,
    cross_q,
    cross_kv,
    cross_o,
    ffn_in,
    ffn_out,
):
    buckets, heads = rel_table.shape
    width = self_q.shape[1]
    length = rel_bucket.shape[0]
    encoded = memory.shape[1]
    model = layer_in.shape[1]
    units = ffn_out.shape[0]
    seqs = seq_len.shape[0]
    half = model // lax.axis_size("mp")
    count = lax.axis_size("dp")
    side = lax.axis_index("mp").astype(jnp.int32).reshape(1)
    index = lax.axis_index("dp").astype(jnp.int32).reshape(1)
    table = jnp.zeros((8, LANES), F32).at[:heads, :buckets].set(rel_table.T)
    kv1 = self_kv.reshape(model, 2 * width)
    kv2 = cross_kv.reshape(model, 2 * width)
    w_in = ffn_in.reshape(model, 2 * units)
    gains = [g.reshape(1, model) for g in (self_gain, cross_gain, ffn_gain)]
    encoder = memory.reshape(seqs * encoded, model)
    across = range(seqs)
    rows = lambda array, s: (array, length, s)
    per = model // count
    ring = ring_orders(count)
    stage1 = []
    for s in across:
        stage1.append(call(
            functools.partial(self_forward, seq=s, width=width), "self_forward",
            [shape((length, model), F32), shape((length, model), BF16), shape((length, 3 * width), BF16),
             shape((length, width), BF16), shape((length, LANES), F32)],
            [seq_len, rows(layer_in, s), gains[0], self_q, kv1, self_o, table, rel_bucket],
            smem=1, keep=(1, 2, 3, 4),
        ))
    swapped1 = [swap(found[0]) for found in stage1]
    encoded_kv = [
        call(project, "encoder_kv", [shape((encoded, 2 * width), BF16)], [rows(encoder, s), kv2])[0]
        for s in across
    ]
    stage2 = []
    for s in across:
        stage2.append(call(
            functools.partial(cross_forward, width=width), "cross_forward",
            [shape((length, model), F32), shape((length, model), F32), shape((length, model), BF16),
             shape((length, width), BF16), shape((length, width), BF16), shape((length, LANES), F32)],
            [rows(layer_in, s), stage1[s][0], swapped1[s], gains[1], cross_q, cross_o, encoded_kv[s]],
            keep=(2, 3, 4, 5),
        ))
    swapped2 = [swap(found[0]) for found in stage2]
    stage3, joint = [], None
    for s in across:
        stage3.append(call(
            ffn_both, "ffn_both",
            [shape((length, half), F32), shape((length, model), F32),
             shape((length, model), BF16), shape((length, units), BF16), shape((length, 2 * units), BF16),
             shape((length, model + half), F32)],
            [side, stage2[s][1], stage2[s][0], swapped2[s], gains[2], rows(grad_out, s), w_in, ffn_out],
            scratch=[pltpu.VMEM((length, model), F32)],
            smem=1, keep=(0, 2, 3, 4), shared=(5, s, joint, seqs),
        ))
        joint = stage3[s][5]
    swapped3 = swap(joint)
    grad3 = joint
    normed3 = [found[2] for found in stage3]
    dgus = [found[4] for found in stage3]
    ffn = Group(index, per, units)
    after = ffn.add(
        [(grad_out, s) for s in across], [found[3] for found in stage3], ring[1], "grad_ffn_out", [joint])
    after = ffn.add(normed3, dgus, ring[0], "grad_gate", after, 0, units)
    after = ffn.add(normed3, dgus, ring[2], "grad_up", after, units, units)
    back_scratch = [
        pltpu.VMEM((length, width), BF16), pltpu.VMEM((width, length), BF16), pltpu.VMEM((width, length), BF16),
        pltpu.VMEM((width, length), F32), pltpu.VMEM((width, length), F32),
    ]
    stage4, joint = [], None
    for s in across:
        stage4.append(call(
            functools.partial(cross_backward, width=width), "cross_backward",
            [shape((length, model), F32), shape((length, model), F32), shape((length, model), BF16),
             shape((length, 3 * width), BF16), shape((encoded, half), F32), shape((1, model), F32),
             shape((encoded, half), F32)],
            [gate(side, *after), rows(grad_out, s), (grad3, length, s, model), (swapped3, length, s, model),
             stage3[s][1], gains[2], stage2[s][3], encoded_kv[s], stage2[s][5], cross_q, kv2, cross_o],
            scratch=back_scratch + [pltpu.VMEM((encoded, model), F32)],
            smem=1, keep=(4, 6), shared=(6, s, joint, seqs),
        ))
        joint = stage4[s][6]
        after = [stage4[s][5]]
    rest4 = joint
    swapped4 = [swap(found[0]) for found in stage4]
    pair = lambda found: [(value, 0) for value in found]
    both = Group(index, per, width + width // 3)
    after, launch = both.add_attention(
        pair([found[2] for found in stage2]), [(encoder, s) for s in across], pair([found[2] for found in stage4]),
        [found[3] for found in stage4], [found[4] for found in stage2], "grad_cross", after)
    after = ffn.step(*after)
    stage5, joint = [], None
    for s in across:
        stage5.append(call(
            functools.partial(self_backward, seq=s, width=width), "self_backward",
            [shape((length, model), F32), shape((length, model), F32), shape((length, model), BF16),
             shape((length, 3 * width), BF16), shape((heads, length, length), BF16), shape((1, model), F32)],
            [gate(seq_len, *after), stage4[s][1], stage4[s][0], swapped4[s],
             stage2[s][1], gains[1], stage1[s][2], stage1[s][4], self_q, kv1, self_o, table, rel_bucket],
            scratch=back_scratch,
            smem=1, shared=(0, s, joint, seqs), direct=s == 0,
        ))
        joint = stage5[s][0]
        after = [stage5[s][5]]
        if s == 0:
            launch(*after, *ffn.arrivals())
    grad5 = joint
    swapped5 = swap(gate(grad5, *both.arrivals()))
    after = ffn.step(*after, *both.arrivals())
    normed1 = pair([found[1] for found in stage1])
    after, launch = both.add_attention(
        normed1, normed1, pair([found[2] for found in stage5]),
        [found[3] for found in stage5], [found[3] for found in stage1], "grad_self", after)
    launch(swapped5, *ffn.arrivals())
    after = ffn.step(swapped5, *after)
    stage6, joint = [], None
    for s in across:
        stage6.append(call(
            input_backward, "input_backward",
            [shape((length, model), F32), shape((1, model), F32)],
            [stage5[s][1], rows(grad5, s), rows(swapped5, s), rows(layer_in, s), gate(gains[0], *after)],
            keep=(0,), shared=(0, s, joint, seqs),
        ))
        joint = stage6[s][0]
        after = [stage6[s][1]]
    grad_layer_in = joint
    swapped6 = swap(gate(rest4, *after))
    spread = call(
        functools.partial(table_backward, buckets=buckets), "table_backward",
        [shape((2 * heads * 8, 8 * buckets), F32)],
        [gate(index, *after), rel_bucket, stage5[0][4], stage5[1][4]],
        scratch=[pltpu.VMEM((2 * heads * 8, 8 * buckets), F32)], smem=1,
    )[0]
    table_grad = spread.reshape(2, heads, 8, 8, buckets).sum(axis=(0, 2, 3)).T
    after = both.step(spread, *ffn.arrivals())
    grad_w_out, grad_gate, grad_up = ffn.finish(spread, *after)
    gain1 = sum(found[1] for found in stage6)
    gain2 = sum(found[5] for found in stage5)
    gain3 = sum(found[5] for found in stage4)
    small = jnp.concatenate([gain1[0], gain2[0], gain3[0], table_grad.reshape(-1)])
    bits = sorted(orders(count)[0], reverse=True)
    arrived = dp_swap(small, bits[0])
    for bit in bits[1:-2]:
        after = both.step(*both.arrivals(), arrived)
        small = small + gate(arrived, *after)
        arrived = dp_swap(small, bit)
    after = both.step(*both.arrivals(), arrived)
    small = small + gate(arrived, *after)
    for bit in bits[-2:]:
        small = small + dp_swap(small, bit)
    theirs3 = gate(swapped3, spread, *after)
    theirs4 = gate(swapped6, *after)
    mixed = jnp.concatenate([found[0] for found in stage3], axis=0)
    mixed = (mixed + theirs3[:, model:]).astype(BF16)
    grad_memory = jnp.concatenate([found[4] for found in stage4], axis=0) + theirs4
    grad_memory = grad_memory.reshape(seqs, encoded, half)
    settled = both.finish()
    results = []
    for first in (0, 3):
        q, k, v = [value[:, :width] for value in settled[first : first + 3]]
        o = jnp.concatenate([value[:, width:] for value in settled[first : first + 3]], axis=1)
        results.append((q, jnp.stack([k, v], axis=1), o))
    (grad_cross_q, grad_cross_kv, grad_cross_o), (grad_self_q, grad_self_kv, grad_self_o) = results
    begin = index[0] * per
    gain_grads = [lax.dynamic_slice_in_dim(small, i * model + begin, per, 0) for i in range(3)]
    grad_table = small[3 * model :].reshape(buckets, heads)
    return (
        mixed,
        grad_layer_in,
        grad_memory,
        *gain_grads,
        grad_table,
        grad_self_q,
        grad_self_kv,
        grad_self_o.T,
        grad_cross_q,
        grad_cross_kv,
        grad_cross_o.T,
        jnp.stack([grad_gate, grad_up], axis=1),
        grad_w_out.T,
    )


def solution(mesh):
    placed = (
        P("dp", None),
        P("dp", None, None),
        P("dp", None),
        P("dp"),
        P(),
        P(),
        P(),
        P(),
        P(None, "mp"),
        P(None, "mp"),
        P(None, None, "mp"),
        P("mp", None),
        P(None, "mp"),
        P(None, None, "mp"),
        P("mp", None),
        P(None, None, "mp"),
        P("mp", None),
    )
    return jax.shard_map(
        on_device,
        mesh=mesh,
        in_specs=placed,
        out_specs=(
            P("dp", "mp"),
            P("dp", None),
            P("dp", None, "mp"),
            P("dp"),
            P("dp"),
            P("dp"),
            P(None, "mp"),
            P("dp", "mp"),
            P("dp", None, "mp"),
            P("mp", "dp"),
            P("dp", "mp"),
            P("dp", None, "mp"),
            P("mp", "dp"),
            P("dp", None, "mp"),
            P("mp", "dp"),
        ),
        check_vma=False,
    )
```
